512 devices in a mesh: dp: 16 (over z_lo, x, core), expert: 32 (over y, z_hi).
Axes of the slice: x: 4, y: 8, z: 8 (z_hi: 4, z_lo: 2; z = z_hi * 2 + z_lo), core: 2. Of those that a mesh axis runs over, the one named last changes fastest.
Arguments:
- tokens: bfloat16 [65536, 4096], P(('dp', 'expert')), may hold values from -6 to 6
- output_gradient: bfloat16 [65536, 4096], P(('dp', 'expert')), may hold values from -6 to 6
- slot: int32 [65536, 4], P(('dp', 'expert')), may hold values from -1 to 7, as said below
- gate_weight: float32 [65536, 4], P(('dp', 'expert')), may hold values from 0.2 to 1
- gate_up_weight: bfloat16 [32, 4096, 384], P('expert', 'dp'), may hold values from -0.09375 to 0.09375
- down_weight: bfloat16 [32, 192, 4096], P('expert', None, 'dp'), may hold values from -0.15625 to 0.15625
Outputs:
- grad_tokens: bfloat16 [65536, 4096], P(('dp', 'expert'))
- grad_gate_up: bfloat16 [32, 4096, 384], P('expert', 'dp')
The draws below stay inside these ranges and needn't reach their ends.
Inputs may be any that keep to these rules, and one draw needn't show every extreme that they name: `slot`: within the tokens of one block of 128 and one window expert, the values other than -1 are 0, 1, ..., k - 1, each once; one window expert, the same one in every block, takes all 8 slots in every block, and each of the other window experts takes at most 4 slots in that block.
All inputs are finite; a program needn't handle non-finite values.
Results may differ from the reference program's by a relative error of at most 0.022.
Values may be sent and summed in bfloat16 or wider, within the bound.
No kernel may reach another device: no remote copies, remote signals or barrier semaphores. Data moves between devices by JAX's collectives and lax.ppermute only.
A program may use at most 64 MiB of HBM per device.

```python
import jax
import jax.numpy as jnp
from jax import lax

D = 4096
F = 1536
GROUP = 8
TOK_DEV = 128
F_DEV = 192
CAP = 8
EXP_WIN = 4
TOKENS = 65536
N_DP = 16
N_EXPERT = 32


def draw_slot(key, part):
    blocks = TOKENS // TOK_DEV
    hot = jax.random.randint(jax.random.fold_in(key, 7), (), 0, EXP_WIN)
    keys = jax.random.split(jax.random.fold_in(key, 11), blocks * EXP_WIN)

    def one_list(sub_key, index):
        expert = index % EXP_WIN
        count_key, order_key = jax.random.split(sub_key)
        count = jax.random.randint(count_key, (), 1, CAP // 2 + 1)
        count = jnp.where(expert == hot, CAP, count)
        order = jax.random.permutation(order_key, TOK_DEV)
        ranks = jnp.argsort(order)
        return jnp.where(ranks < count, ranks, -1).astype(jnp.int32)
    lists = jax.vmap(one_list)(keys, jnp.arange(blocks * EXP_WIN, dtype=jnp.int32))
    return jnp.transpose(lists.reshape(blocks, EXP_WIN, TOK_DEV), (0, 2, 1)).reshape(TOKENS, EXP_WIN)


def levels(own_key, dims, cuts, smallest, high):
    factor_of = 1.0
    for dim, parts in cuts:
        heights = jax.random.uniform(jax.random.fold_in(jax.random.fold_in(own_key, 6), dim), (parts,), jnp.float32, smallest / len(cuts), high / len(cuts))
        factor_of = factor_of * jnp.repeat(jnp.exp(heights), dims[dim] // parts).reshape((-1,) + (1,) * (len(dims) - 1 - dim))
    return factor_of


def normal_values(key, dims, scale, most, cuts=(), kind=jnp.bfloat16):
    array = jax.random.normal(key, dims, jnp.float32) * scale
    if len(cuts) > 0:
        array = levels(key, dims, cuts, -0.22, 0.18) * array
    return jnp.clip(array, min=-most, max=most).astype(kind)


def setup_inputs(seed: int = 0) -> dict:
    key_of = jax.random.split(jax.random.key(seed), 7)
    tokens = normal_values(key_of[0], (TOKENS, D), 1.0, 6.0, ((0, 512),))
    output_gradient = normal_values(key_of[1], (TOKENS, D), 1.0, 6.0, ((0, 512),))
    slot = draw_slot(jax.random.fold_in(key_of[6], 71), 0)
    gate_weight = jnp.clip(0.2 + 0.8 * jax.random.uniform(key_of[3], (TOKENS, EXP_WIN), jnp.float32) ** levels(key_of[3], (TOKENS, EXP_WIN), ((0, 512),), -0.2, 0.2), 0.2, 1.0)
    gate_up_weight = normal_values(key_of[4], (N_EXPERT, D, 2 * F_DEV), D ** -0.5, 0.09375, ((0, 32), (1, 16)))
    down_weight = normal_values(key_of[5], (N_EXPERT, F_DEV, D), F ** -0.5, 0.15625, ((0, 32), (2, 16)))
    return {"tokens": tokens, "output_gradient": output_gradient, "slot": slot, "gate_weight": gate_weight, "gate_up_weight": gate_up_weight, "down_weight": down_weight}


def expert_slice(x_mat, g_mat, gate_up, down):
    joined = jnp.dot(x_mat, gate_up, preferred_element_type=jnp.float32)
    half = gate_up.shape[1] // 2
    pre = joined[:, :half]
    up = joined[:, half:]
    sig = jax.nn.sigmoid(pre)
    act = pre * sig
    dh = lax.dot_general(g_mat, down, (((1,), (1,)), ((), ())), preferred_element_type=jnp.float32)
    dgate = dh * up * sig * (1.0 + pre * (1.0 - sig))
    dup = dh * act
    dgu = jnp.concatenate([dgate, dup], axis=1).astype(jnp.bfloat16)
    dx_part = lax.dot_general(dgu, gate_up, (((1,), (1,)), ((), ())), preferred_element_type=jnp.float32).astype(jnp.bfloat16)
    part_gu = lax.dot_general(x_mat, dgu, (((0,), (0,)), ((), ())), preferred_element_type=jnp.float32).astype(jnp.bfloat16)
    return dx_part, part_gu


def reference(tokens, output_gradient, slot, gate_weight, gate_up_weight, down_weight):
    x_all = tokens.reshape(N_DP, N_EXPERT, TOK_DEV, D)
    g_all = output_gradient.reshape(N_DP, N_EXPERT, TOK_DEV, D)
    s_all = slot.reshape(N_DP, N_EXPERT, TOK_DEV, EXP_WIN)
    w_all = gate_weight.reshape(N_DP, N_EXPERT, TOK_DEV, EXP_WIN)
    positions = jnp.arange(CAP, dtype=jnp.int32)

    def per_replica(acc_gu, inputs):
        x_d, g_d, s_d, down_matrix = inputs
        selector = jnp.transpose(s_d, (0, 2, 1))[:, :, None, :] == positions[None, None, :, None]
        picked_experts = selector.astype(jnp.float32)
        rows_x = jnp.einsum('iect,itd->iecd', picked_experts, x_d.astype(jnp.float32)).astype(jnp.bfloat16)
        rows_dy = jnp.einsum('iect,itd->iecd', picked_experts, g_d.astype(jnp.float32))
        selected_gate = jnp.einsum('ovjb,obv->ovj', picked_experts, down_matrix)
        rows_g = (rows_dy * selected_gate[..., None]).astype(jnp.bfloat16)
        grad_x = jnp.zeros((N_EXPERT, TOK_DEV, D), jnp.float32)
        parts_gu = []
        for expert in range(EXP_WIN):
            x_mat = rows_x[:, expert].reshape(N_EXPERT * CAP, D)
            g_mat = rows_g[:, expert].reshape(N_EXPERT * CAP, D)
            total = jnp.zeros((N_EXPERT * CAP, D), jnp.float32)
            for piece in range(GROUP):
                index = expert * GROUP + piece
                dx_part, part_gu = expert_slice(x_mat, g_mat, gate_up_weight[index], down_weight[index])
                total = total + lax.optimization_barrier(dx_part).astype(jnp.float32)
                parts_gu.append(lax.optimization_barrier(part_gu).astype(jnp.float32))
            grad_x = grad_x + jnp.einsum('ict,icd->itd', picked_experts[:, expert], total.reshape(N_EXPERT, CAP, D))
        acc_gu = acc_gu + jnp.stack(parts_gu)
        return acc_gu, grad_x.astype(jnp.bfloat16)

    start = jnp.zeros((N_EXPERT, D, 2 * F_DEV), jnp.float32)
    acc_gu, grad_x = lax.scan(per_replica, start, (x_all, g_all, s_all, w_all))
    grad_tokens = grad_x.reshape(TOKENS, D)
    return grad_tokens, acc_gu.astype(jnp.bfloat16)
```

```python
import jax
import jax.numpy as jnp
from jax import lax
from jax.sharding import Mesh, PartitionSpec as P

FINE = ("zl", "x", "c", "yh", "yl", "zh")
EXPERT = ("yh", "yl", "zh")
CAP = 8
LANE = 128


def f32_dot(a, b, dims):
    return lax.dot_general(a, b, (dims, ((), ())), preferred_element_type=jnp.float32)


def a2a(v, axes):
    return lax.all_to_all(v, axes, split_axis=0, concat_axis=0, tiled=True)


def swap_pairs(v, axis):
    return lax.ppermute(v, axis, [(0, 1), (1, 0)])


def on_device(tokens, output_gradient, slot, gate_weight, gate_up_weight, down_weight):
    n_win = slot.shape[1]
    width = tokens.shape[1]
    n_half = width // (2 * LANE)
    hid = down_weight.shape[1]
    n_yl, n_zh = lax.axis_size("yl"), lax.axis_size("zh")

    w_own = jnp.concatenate([gate_up_weight[0], jnp.transpose(down_weight[0])], axis=1)
    w_pair = a2a(w_own.reshape(n_yl, LANE, 3 * hid), "yl")
    w_mine = jnp.transpose(w_pair.reshape(n_yl, LANE, 3, hid), (1, 2, 0, 3)).reshape(LANE, 3 * n_yl * hid)
    w_full = lax.all_gather(w_mine, ("zl", "x", "c"), axis=0, tiled=True)
    gu_cols = 2 * n_yl * hid
    w_gu, w_down = w_full[:, :gu_cols], w_full[:, gu_cols:]

    positions = jnp.arange(CAP, dtype=jnp.int32)
    selector = jnp.transpose(slot)[:, None, :] == positions[None, :, None]
    picked = selector.astype(jnp.bfloat16)
    rows_x = jnp.einsum("ect,td->ecd", picked, tokens, preferred_element_type=jnp.float32).astype(jnp.bfloat16)
    rows_dy = jnp.einsum("ect,td->ecd", picked, output_gradient, preferred_element_type=jnp.float32)
    gate = jnp.sum(jnp.where(selector, jnp.transpose(gate_weight)[:, None, :], 0.0), axis=2)
    rows_g = (rows_dy * gate[..., None]).astype(jnp.bfloat16)
    rows = jnp.concatenate([rows_x, rows_g], axis=1).reshape(n_win, 2 * CAP, n_half, n_yl, LANE)
    rows = jnp.transpose(rows, (0, 3, 1, 2, 4)).reshape(n_win, n_yl, 1, 2 * CAP, n_half * LANE)
    rows = jnp.broadcast_to(rows, (n_win, n_yl, n_zh, 2 * CAP, n_half * LANE))
    recv = a2a(rows.reshape(-1, 2 * CAP, n_half * LANE), EXPERT)
    n_src = recv.shape[0]
    x_mat = recv[:, :CAP].reshape(n_src * CAP, n_half * LANE)
    g_mat = recv[:, CAP:].reshape(n_src * CAP, n_half * LANE)

    part = jnp.concatenate(
        [f32_dot(x_mat, w_gu, ((1,), (0,))), f32_dot(g_mat, w_down, ((1,), (0,)))], axis=1
    ).astype(jnp.bfloat16)
    total = part.astype(jnp.float32) + swap_pairs(part, "yl").astype(jnp.float32)
    pre, up, dh = jnp.split(total, 3, axis=1)
    sig = jax.nn.sigmoid(pre)
    dgate = dh * up * sig * (1.0 + pre * (1.0 - sig))
    dup = dh * (pre * sig)
    dgu = jnp.concatenate([dgate, dup], axis=1).astype(jnp.bfloat16)

    dx = f32_dot(dgu, w_gu, ((1,), (1,))).astype(jnp.bfloat16)
    pgu = f32_dot(x_mat, dgu, ((0,), (0,))).astype(jnp.bfloat16)

    n_c = lax.axis_size("c")
    pgu = jnp.transpose(pgu.reshape(-1, n_c, LANE, gu_cols), (1, 0, 2, 3))
    both = a2a(pgu, "c").astype(jnp.float32)
    chip = (both[0] + both[1]).astype(jnp.bfloat16)
    summed = jnp.sum(a2a(chip, ("zl", "x")).astype(jnp.float32), axis=0).astype(jnp.bfloat16)
    summed = jnp.transpose(summed.reshape(LANE, 2, n_yl, hid), (2, 0, 1, 3)).reshape(n_yl, LANE, 2 * hid)
    grad_gu = a2a(summed, "yl").reshape(1, n_yl * LANE, 2 * hid)

    back = a2a(dx.reshape(n_src, CAP, n_half * LANE), EXPERT)
    back = jnp.sum(back.reshape(n_win, n_yl, n_zh, CAP, n_half, LANE).astype(jnp.float32), axis=2)
    back = jnp.transpose(back, (0, 2, 3, 1, 4)).reshape(n_win, CAP, width)
    grad_tokens = jnp.einsum("ect,ecd->td", selector.astype(jnp.float32), back).astype(jnp.bfloat16)
    return grad_tokens, grad_gu


def solution(mesh):
    fine = Mesh(mesh.devices.reshape(2, 4, 2, 4, 2, 4), FINE)
    dp, ex = FINE[:3], FINE[3:]
    in_specs = (P(FINE, None), P(FINE, None), P(FINE, None), P(FINE, None), P(ex, dp, None), P(ex, None, dp))
    out_specs = (P(FINE, None), P(ex, dp, None))
    return jax.shard_map(on_device, mesh=fine, in_specs=in_specs, out_specs=out_specs, check_vma=False)
```

```python
import jax
import jax.numpy as jnp
from jax import lax
from jax.sharding import Mesh, PartitionSpec as P

FINE = ("zl", "x", "c", "yh", "yl", "zh")
EXPERT = ("yh", "yl", "zh")
CAP = 8
LANE = 128


def f32_dot(a, b, dims):
    return lax.dot_general(a, b, (dims, ((), ())), preferred_element_type=jnp.float32)


def a2a(v, axes):
    return lax.all_to_all(v, axes, split_axis=0, concat_axis=0, tiled=True)


def swap_pairs(v, axis):
    return lax.ppermute(v, axis, [(0, 1), (1, 0)])


def on_device(tokens, output_gradient, slot, gate_weight, gate_up_weight, down_weight):
    n_win = slot.shape[1]
    width = tokens.shape[1]
    n_half = width // (2 * LANE)
    hid = down_weight.shape[1]
    n_yl, n_zh = lax.axis_size("yl"), lax.axis_size("zh")

    n_zl = lax.axis_size("zl")
    w_own = jnp.concatenate([gate_up_weight[0], jnp.transpose(down_weight[0])], axis=1)
    w_sent = jnp.broadcast_to(w_own.reshape(1, n_yl, LANE, 3 * hid), (n_zl, n_yl, LANE, 3 * hid))
    w_pair = a2a(w_sent.reshape(n_zl * n_yl, LANE, 3 * hid), ("zl", "yl"))
    w_mine = jnp.transpose(w_pair.reshape(n_zl, n_yl, LANE, 3, hid), (0, 2, 3, 1, 4))
    w_full = lax.all_gather(w_mine.reshape(n_zl * LANE, 3 * n_yl * hid), ("x", "c"), axis=0, tiled=True)
    gu_cols = 2 * n_yl * hid
    w_gu, w_down = w_full[:, :gu_cols], w_full[:, gu_cols:]

    positions = jnp.arange(CAP, dtype=jnp.int32)
    selector = jnp.transpose(slot)[:, None, :] == positions[None, :, None]
    picked = selector.astype(jnp.bfloat16)
    rows_x = jnp.einsum("ect,td->ecd", picked, tokens, preferred_element_type=jnp.float32).astype(jnp.bfloat16)
    rows_dy = jnp.einsum("ect,td->ecd", picked, output_gradient, preferred_element_type=jnp.float32)
    gate = jnp.sum(jnp.where(selector, jnp.transpose(gate_weight)[:, None, :], 0.0), axis=2)
    rows_g = (rows_dy * gate[..., None]).astype(jnp.bfloat16)
    n_xc = n_half // n_zl
    rows = jnp.concatenate([rows_x, rows_g], axis=1).reshape(n_win, 2 * CAP, n_zl, n_xc, n_yl, LANE)
    rows = jnp.transpose(rows, (0, 4, 1, 3, 2, 5)).reshape(n_win, n_yl, 1, 2 * CAP, n_half * LANE)
    rows = jnp.broadcast_to(rows, (n_win, n_yl, n_zh, 2 * CAP, n_half * LANE))
    recv = a2a(rows.reshape(-1, 2 * CAP, n_half * LANE), EXPERT)
    n_src = recv.shape[0]
    x_mat = recv[:, :CAP].reshape(n_src * CAP, n_half * LANE)
    g_mat = recv[:, CAP:].reshape(n_src * CAP, n_half * LANE)

    part = jnp.concatenate(
        [f32_dot(x_mat, w_gu, ((1,), (0,))), f32_dot(g_mat, w_down, ((1,), (0,)))], axis=1
    ).astype(jnp.bfloat16)
    total = part.astype(jnp.float32) + swap_pairs(part, "yl").astype(jnp.float32)
    pre, up, dh = jnp.split(total, 3, axis=1)
    sig = jax.nn.sigmoid(pre)
    dgate = dh * up * sig * (1.0 + pre * (1.0 - sig))
    dup = dh * (pre * sig)
    dgu = jnp.concatenate([dgate, dup], axis=1).astype(jnp.bfloat16)

    dx = f32_dot(dgu, w_gu, ((1,), (1,))).astype(jnp.bfloat16)
    pgu = f32_dot(x_mat, dgu, ((0,), (0,))).astype(jnp.bfloat16)

    summed = lax.psum_scatter(pgu, ("x", "c"), scatter_dimension=0, tiled=True)
    summed = jnp.transpose(summed.reshape(n_zl, LANE, 2, n_yl, hid), (0, 3, 1, 2, 4))
    summed = a2a(summed.reshape(n_zl * n_yl, LANE, 2 * hid), ("zl", "yl"))
    grad_gu = jnp.sum(summed.reshape(n_zl, n_yl * LANE, 2 * hid).astype(jnp.float32), axis=0)
    grad_gu = grad_gu.astype(jnp.bfloat16)[None]

    back = a2a(dx.reshape(n_src, CAP, n_half * LANE), EXPERT)
    back = jnp.sum(back.reshape(n_win, n_yl, n_zh, CAP, n_xc, n_zl, LANE).astype(jnp.float32), axis=2)
    back = jnp.transpose(back, (0, 2, 4, 3, 1, 5)).reshape(n_win, CAP, width)
    grad_tokens = jnp.einsum("ect,ecd->td", selector.astype(jnp.float32), back).astype(jnp.bfloat16)
    return grad_tokens, grad_gu


def solution(mesh):
    fine = Mesh(mesh.devices.reshape(2, 4, 2, 4, 2, 4), FINE)
    dp, ex = FINE[:3], FINE[3:]
    in_specs = (P(FINE, None), P(FINE, None), P(FINE, None), P(FINE, None), P(ex, dp, None), P(ex, None, dp))
    out_specs = (P(FINE, None), P(ex, dp, None))
    return jax.shard_map(on_device, mesh=fine, in_specs=in_specs, out_specs=out_specs, check_vma=False)
```

```python
import jax
import jax.numpy as jnp
from jax import lax
from jax.experimental import pallas as pl
from jax.experimental.pallas import tpu as pltpu
from jax.sharding import Mesh, PartitionSpec as P

FINE = ("zl", "x", "c", "yh", "yl", "zh")
EXPERT = ("yh", "yl", "zh")
CAP = 8
LANE = 128


def f32_dot(a, b, dims):
    return lax.dot_general(a, b, (dims, ((), ())), preferred_element_type=jnp.float32)


def a2a(v, axes):
    return lax.all_to_all(v, axes, split_axis=0, concat_axis=0, tiled=True)


def swap(v, flip):
    return lax.ppermute(v, ("zl", "yl"), [(i, i ^ flip) for i in range(4)])


def part_kernel(gu_cols, w_ref, first_ref, rest_ref, part_ref, acc_gu, acc_dh):
    step = pl.program_id(0)

    def products(rows_ref):
        n_src, _, depth = rows_ref.shape
        x = rows_ref[:, :CAP, :].reshape(n_src * CAP, depth)
        g = rows_ref[:, CAP:, :].reshape(n_src * CAP, depth)
        gu = jnp.dot(x, w_ref[:, :gu_cols], preferred_element_type=jnp.float32)
        return gu, jnp.dot(g, w_ref[:, gu_cols:], preferred_element_type=jnp.float32)

    @pl.when(step == 0)
    def _():
        acc_gu[...], acc_dh[...] = products(first_ref)

    @pl.when(step > 0)
    def _():
        gu, dh = products(rest_ref)
        acc_gu[...] += gu
        acc_dh[...] += dh

    @pl.when(step == pl.num_programs(0) - 1)
    def _():
        part_ref[:, :gu_cols] = acc_gu[...].astype(part_ref.dtype)
        part_ref[:, gu_cols:] = acc_dh[...].astype(part_ref.dtype)


def row_specs(first, rest):
    n_src, rows, depth = first.shape
    return [
        pl.BlockSpec((n_src, rows, depth), lambda k: (0, 0, 0)),
        pl.BlockSpec((n_src, rows, depth), lambda k: (0, 0, jnp.maximum(k - 1, 0))),
    ]


def partial_products(w_full, first, rest, gu_cols):
    n_src, _, depth = first.shape
    width, cols = w_full.shape
    m = n_src * CAP
    return pl.pallas_call(
        lambda *refs: part_kernel(gu_cols, *refs),
        grid=(width // depth,),
        in_specs=[pl.BlockSpec((depth, cols), lambda k: (k, 0)), *row_specs(first, rest)],
        out_specs=pl.BlockSpec((m, cols), lambda k: (0, 0)),
        out_shape=jax.ShapeDtypeStruct((m, cols), jnp.bfloat16),
        scratch_shapes=[pltpu.VMEM((m, gu_cols), jnp.float32), pltpu.VMEM((m, cols - gu_cols), jnp.float32)],
        name="partial_products",
    )(w_full, first, rest)


def pgu_kernel(dgu_ref, first_ref, rest_ref, pgu_ref):
    def product(rows_ref):
        n_src, _, depth = rows_ref.shape
        x = rows_ref[:, :CAP, :].reshape(n_src * CAP, depth)
        pgu_ref[...] = f32_dot(x, dgu_ref[...], ((0,), (0,))).astype(pgu_ref.dtype)

    pl.when(pl.program_id(0) == 0)(lambda: product(first_ref))
    pl.when(pl.program_id(0) > 0)(lambda: product(rest_ref))


def weight_products(dgu, first, rest):
    depth = first.shape[2]
    width = depth + rest.shape[2]
    m, cols = dgu.shape
    return pl.pallas_call(
        pgu_kernel,
        grid=(width // depth,),
        in_specs=[pl.BlockSpec((m, cols), lambda k: (0, 0)), *row_specs(first, rest)],
        out_specs=pl.BlockSpec((depth, cols), lambda k: (k, 0)),
        out_shape=jax.ShapeDtypeStruct((width, cols), jnp.bfloat16),
        name="weight_products",
    )(dgu, first, rest)


def dx_kernel(dgu_ref, w_ref, dx_ref):
    gu_cols = dgu_ref.shape[1]
    dx_ref[...] = f32_dot(dgu_ref[...], w_ref[:, :gu_cols], ((1,), (1,))).astype(dx_ref.dtype)


def input_products(dgu, w_full, depth=512):
    m, cols = dgu.shape
    width, all_cols = w_full.shape
    return pl.pallas_call(
        dx_kernel,
        grid=(width // depth,),
        in_specs=[pl.BlockSpec((m, cols), lambda k: (0, 0)), pl.BlockSpec((depth, all_cols), lambda k: (k, 0))],
        out_specs=pl.BlockSpec((m, depth), lambda k: (0, k)),
        out_shape=jax.ShapeDtypeStruct((m, width), jnp.bfloat16),
        name="input_products",
    )(dgu, w_full)


def on_device(tokens, output_gradient, slot, gate_weight, gate_up_weight, down_weight):
    n_win = slot.shape[1]
    width = tokens.shape[1]
    n_half = width // (2 * LANE)
    hid = down_weight.shape[1]
    n_yl, n_zh = lax.axis_size("yl"), lax.axis_size("zh")

    n_zl = lax.axis_size("zl")
    n_xc = n_half // n_zl
    positions = jnp.arange(CAP, dtype=jnp.int32)
    selector = jnp.transpose(slot)[:, None, :] == positions[None, :, None]
    picked = selector.astype(jnp.bfloat16)
    rows_x = jnp.einsum("ect,td->ecd", picked, tokens, preferred_element_type=jnp.float32).astype(jnp.bfloat16)
    rows_dy = jnp.einsum("ect,td->ecd", picked, output_gradient, preferred_element_type=jnp.float32)
    gate = jnp.sum(jnp.where(selector, jnp.transpose(gate_weight)[:, None, :], 0.0), axis=2)
    rows_g = (rows_dy * gate[..., None]).astype(jnp.bfloat16)
    rows = jnp.concatenate([rows_x, rows_g], axis=1).reshape(n_win, 2 * CAP, n_zl, n_xc, n_yl, LANE)
    rows = jnp.transpose(rows, (0, 4, 1, 3, 2, 5)).reshape(n_win, n_yl, 1, 2 * CAP, n_half * LANE)
    rows = jnp.broadcast_to(rows, (n_win, n_yl, n_zh, 2 * CAP, n_half * LANE))
    rows = rows.reshape(-1, 2 * CAP, n_half * LANE)
    cut = n_half * LANE // 4
    first = a2a(rows[:, :, :cut], EXPERT)

    zl, yl = lax.axis_index("zl"), lax.axis_index("yl")
    w_own = jnp.concatenate([gate_up_weight[0], jnp.transpose(down_weight[0])], axis=1)
    kept = lax.dynamic_slice_in_dim(w_own, yl * LANE, LANE, axis=0)
    given = lax.dynamic_slice_in_dim(w_own, (1 - yl) * LANE, LANE, axis=0)
    w_got = [kept, swap(given, 1), swap(kept, 2), swap(given, 3)]

    def w_of(zl_src, yl_src):
        same_zl, same_yl = zl == zl_src, yl == yl_src
        return jnp.where(same_zl, jnp.where(same_yl, w_got[0], w_got[1]), jnp.where(same_yl, w_got[2], w_got[3]))

    w_rows = []
    for zl_src in range(n_zl):
        w0, w1 = w_of(zl_src, 0), w_of(zl_src, 1)
        w_rows.append(jnp.concatenate([w0[:, : 2 * hid], w1[:, : 2 * hid], w0[:, 2 * hid :], w1[:, 2 * hid :]], axis=1))
    w_mine = jnp.concatenate(w_rows, axis=0)
    first, rows_rest, w_mine = lax.optimization_barrier((first, rows[:, :, cut:], w_mine))
    w_full = lax.all_gather(w_mine, ("x", "c"), axis=0, tiled=True)
    gu_cols = 2 * n_yl * hid
    rest = a2a(rows_rest, EXPERT)
    n_src = first.shape[0]

    part = partial_products(w_full, first, rest, gu_cols)
    total = part.astype(jnp.float32) + swap(part, 1).astype(jnp.float32)
    dgu = []
    for i in range(n_yl):
        pre, up = total[:, 2 * i * hid : (2 * i + 1) * hid], total[:, (2 * i + 1) * hid : (2 * i + 2) * hid]
        dh = total[:, gu_cols + i * hid : gu_cols + (i + 1) * hid]
        sig = jax.nn.sigmoid(pre)
        dgu += [dh * up * sig * (1.0 + pre * (1.0 - sig)), dh * (pre * sig)]
    dgu = jnp.concatenate(dgu, axis=1).astype(jnp.bfloat16)

    pgu = weight_products(dgu, first, rest)
    dx = input_products(dgu, w_full)

    summed = lax.psum_scatter(pgu, ("x", "c"), scatter_dimension=0, tiled=True)
    summed = jnp.transpose(summed.reshape(n_zl, LANE, n_yl, 2 * hid), (0, 2, 1, 3))
    summed = a2a(summed.reshape(n_zl * n_yl, LANE, 2 * hid), ("zl", "yl"))
    grad_gu = jnp.sum(summed.reshape(n_zl, n_yl * LANE, 2 * hid).astype(jnp.float32), axis=0)
    grad_gu = grad_gu.astype(jnp.bfloat16)[None]

    back = a2a(dx.reshape(n_src, CAP, n_half * LANE), EXPERT)
    back = jnp.sum(back.reshape(n_win, n_yl, n_zh, CAP, n_xc, n_zl, LANE).astype(jnp.float32), axis=2)
    back = jnp.transpose(back, (0, 2, 4, 3, 1, 5)).reshape(n_win, CAP, width)
    grad_tokens = jnp.einsum("ect,ecd->td", selector.astype(jnp.float32), back).astype(jnp.bfloat16)
    return grad_tokens, grad_gu


def solution(mesh):
    fine = Mesh(mesh.devices.reshape(2, 4, 2, 4, 2, 4), FINE)
    dp, ex = FINE[:3], FINE[3:]
    in_specs = (P(FINE, None), P(FINE, None), P(FINE, None), P(FINE, None), P(ex, dp, None), P(ex, None, dp))
    out_specs = (P(FINE, None), P(ex, dp, None))
    return jax.shard_map(on_device, mesh=fine, in_specs=in_specs, out_specs=out_specs, check_vma=False)
```

```python
import jax
import jax.numpy as jnp
from jax import lax
from jax.experimental import pallas as pl
from jax.experimental.pallas import tpu as pltpu
from jax.sharding import Mesh, PartitionSpec as P

FINE = ("zl", "x", "c", "yh", "yl", "zh")
EXPERT = ("yh", "yl", "zh")
CAP = 8
LANE = 128


def f32_dot(a, b, dims):
    return lax.dot_general(a, b, (dims, ((), ())), preferred_element_type=jnp.float32)


def a2a(v, axes):
    return lax.all_to_all(v, axes, split_axis=0, concat_axis=0, tiled=True)


def swap(v, axis):
    return lax.ppermute(v, axis, [(0, 1), (1, 0)])


def split_kernel(core_ref, rows_ref, kept_ref, given_ref):
    n_src, _, depth = rows_ref.shape
    x = rows_ref[:, :CAP, :].reshape(n_src * CAP, depth)
    low, high = x[:, : depth // 2].T, x[:, depth // 2 :].T

    @pl.when(core_ref[0] == 0)
    def _():
        kept_ref[...], given_ref[...] = low, high

    @pl.when(core_ref[0] != 0)
    def _():
        kept_ref[...], given_ref[...] = high, low


def split_rows(core, recv, depth):
    n_src, rows, width = recv.shape
    out = jax.ShapeDtypeStruct((width // 2, n_src * CAP), recv.dtype)
    out_spec = pl.BlockSpec((depth // 2, n_src * CAP), lambda k: (k, 0))
    return pl.pallas_call(
        split_kernel,
        grid=(width // depth,),
        in_specs=[
            pl.BlockSpec(memory_space=pltpu.SMEM),
            pl.BlockSpec((n_src, rows, depth), lambda k: (0, 0, k)),
        ],
        out_specs=[out_spec, out_spec],
        out_shape=[out, out],
        name="split_rows",
    )(core.reshape(1), recv)


def pgu_kernel(xa_ref, xb_ref, dgu_a_ref, dgu_b_ref, pgu_ref):
    acc = jnp.dot(xa_ref[...], dgu_a_ref[...], preferred_element_type=jnp.float32)
    acc += jnp.dot(xb_ref[...], dgu_b_ref[...], preferred_element_type=jnp.float32)
    n_zl, n_yl, lanes, cols = pgu_ref.shape
    for i in range(n_zl):
        for j in range(n_yl):
            block = acc[i * lanes : (i + 1) * lanes, j * cols : (j + 1) * cols]
            pgu_ref[i, j] = block.astype(pgu_ref.dtype)


def weight_products(xt_a, xt_b, dgu_a, dgu_b, n_zl, n_yl):
    width, m = xt_a.shape
    cols = dgu_a.shape[1] // n_yl
    x_spec = pl.BlockSpec((n_zl * LANE, m), lambda k: (k, 0))
    dgu_spec = pl.BlockSpec(dgu_a.shape, lambda k: (0, 0))
    n_x = width // (n_zl * LANE)
    out = pl.pallas_call(
        pgu_kernel,
        grid=(n_x,),
        in_specs=[x_spec, x_spec, dgu_spec, dgu_spec],
        out_specs=pl.BlockSpec((None, n_zl, n_yl, LANE, cols), lambda k: (k, 0, 0, 0, 0)),
        out_shape=jax.ShapeDtypeStruct((n_x, n_zl, n_yl, LANE, cols), jnp.bfloat16),
        name="weight_products",
    )(xt_a, xt_b, dgu_a, dgu_b)
    return out.reshape(-1, cols)


def on_device(tokens, output_gradient, slot, gate_weight, gate_up_weight, down_weight):
    n_win = slot.shape[1]
    width = tokens.shape[1]
    n_half = width // (2 * LANE)
    hid = down_weight.shape[1]
    n_yl, n_zh, n_c = lax.axis_size("yl"), lax.axis_size("zh"), lax.axis_size("c")

    n_zl = lax.axis_size("zl")
    w_own = jnp.concatenate([gate_up_weight[0], jnp.transpose(down_weight[0])], axis=1)
    w_sent = jnp.broadcast_to(w_own.reshape(1, n_yl, LANE, 3 * hid), (n_zl, n_yl, LANE, 3 * hid))
    w_pair = a2a(w_sent.reshape(n_zl * n_yl, LANE, 3 * hid), ("zl", "yl"))
    w_pair = w_pair.reshape(n_zl, n_yl, LANE, 3 * hid)
    w_mine = [w_pair[:, i, :, : 2 * hid] for i in range(n_yl)] + [w_pair[:, i, :, 2 * hid :] for i in range(n_yl)]
    w_mine = jnp.concatenate(w_mine, axis=2).reshape(n_zl * LANE, 3 * n_yl * hid)
    w_full = lax.all_gather(w_mine, ("x", "c"), axis=0, tiled=True)
    gu_cols = 2 * n_yl * hid
    w_gu, w_down = w_full[:, :gu_cols], w_full[:, gu_cols:]

    positions = jnp.arange(CAP, dtype=jnp.int32)
    selector = jnp.transpose(slot)[:, None, :] == positions[None, :, None]
    picked = selector.astype(jnp.bfloat16)
    rows_x = jnp.einsum("ect,td->ecd", picked, tokens, preferred_element_type=jnp.float32).astype(jnp.bfloat16)
    rows_dy = jnp.einsum("ect,td->ecd", picked, output_gradient, preferred_element_type=jnp.float32)
    gate = jnp.sum(jnp.where(selector, jnp.transpose(gate_weight)[:, None, :], 0.0), axis=2)
    rows_g = (rows_dy * gate[..., None]).astype(jnp.bfloat16)
    n_xc = n_half // n_zl
    rows = jnp.concatenate([rows_x, rows_g], axis=1).reshape(n_win, 2 * CAP, n_zl, n_xc, n_yl, LANE)
    rows = jnp.transpose(rows, (0, 4, 1, 3, 2, 5)).reshape(n_win, n_yl, 1, 2 * CAP, n_half * LANE)
    rows = jnp.broadcast_to(rows, (n_win, n_yl, n_zh, 2 * CAP, n_half * LANE))
    recv = a2a(rows.reshape(-1, 2 * CAP, n_half * LANE), EXPERT)
    n_src = recv.shape[0]
    x_mat = recv[:, :CAP].reshape(n_src * CAP, n_half * LANE)
    g_mat = recv[:, CAP:].reshape(n_src * CAP, n_half * LANE)

    part = jnp.concatenate(
        [f32_dot(x_mat, w_gu, ((1,), (0,))), f32_dot(g_mat, w_down, ((1,), (0,)))], axis=1
    ).astype(jnp.bfloat16)

    xt_kept, xt_given = split_rows(lax.axis_index("c"), recv, n_c * n_zl * LANE)
    part_other, xt_kept, xt_got = lax.optimization_barrier((swap(part, "yl"), xt_kept, swap(xt_given, "c")))

    total = part.astype(jnp.float32) + part_other.astype(jnp.float32)
    dgu = []
    for i in range(n_yl):
        pre, up = total[:, 2 * i * hid : (2 * i + 1) * hid], total[:, (2 * i + 1) * hid : (2 * i + 2) * hid]
        dh = total[:, gu_cols + i * hid : gu_cols + (i + 1) * hid]
        sig = jax.nn.sigmoid(pre)
        dgu += [dh * up * sig * (1.0 + pre * (1.0 - sig)), dh * (pre * sig)]
    dgu = jnp.concatenate(dgu, axis=1).astype(jnp.bfloat16)

    dx = f32_dot(dgu, w_gu, ((1,), (1,))).astype(jnp.bfloat16)
    dx, dgu_other = lax.optimization_barrier((dx, swap(dgu, "c")))
    pgu = weight_products(xt_kept, xt_got, dgu, dgu_other, n_zl, n_yl)

    summed = lax.psum_scatter(pgu, "x", scatter_dimension=0, tiled=True)
    summed = a2a(summed.reshape(n_zl * n_yl, LANE, 2 * hid), ("zl", "yl"))
    grad_gu = jnp.sum(summed.reshape(n_zl, n_yl * LANE, 2 * hid).astype(jnp.float32), axis=0)
    grad_gu = grad_gu.astype(jnp.bfloat16)[None]

    back = a2a(dx.reshape(n_src, CAP, n_half * LANE), EXPERT)
    back = jnp.sum(back.reshape(n_win, n_yl, n_zh, CAP, n_xc, n_zl, LANE).astype(jnp.float32), axis=2)
    back = jnp.transpose(back, (0, 2, 4, 3, 1, 5)).reshape(n_win, CAP, width)
    grad_tokens = jnp.einsum("ect,ecd->td", selector.astype(jnp.float32), back).astype(jnp.bfloat16)
    return grad_tokens, grad_gu


def solution(mesh):
    fine = Mesh(mesh.devices.reshape(2, 4, 2, 4, 2, 4), FINE)
    dp, ex = FINE[:3], FINE[3:]
    in_specs = (P(FINE, None), P(FINE, None), P(FINE, None), P(FINE, None), P(ex, dp, None), P(ex, None, dp))
    out_specs = (P(FINE, None), P(ex, dp, None))
    return jax.shard_map(on_device, mesh=fine, in_specs=in_specs, out_specs=out_specs, check_vma=False)
```

```python
import jax
import jax.numpy as jnp
from jax import lax
from jax.sharding import Mesh, PartitionSpec as P

FINE = ("zl", "x", "c", "yh", "yl", "zh")
EXPERT = ("yh", "yl", "zh")
CAP = 8
LANE = 128


def f32_dot(a, b, dims):
    return lax.dot_general(a, b, (dims, ((), ())), preferred_element_type=jnp.float32)


def a2a(v, axes):
    return lax.all_to_all(v, axes, split_axis=0, concat_axis=0, tiled=True)


def swap(v, axis):
    return lax.ppermute(v, axis, [(0, 1), (1, 0)])


def on_device(tokens, output_gradient, slot, gate_weight, gate_up_weight, down_weight):
    n_win = slot.shape[1]
    width = tokens.shape[1]
    n_half = width // (2 * LANE)
    hid = down_weight.shape[1]
    n_yl, n_zh = lax.axis_size("yl"), lax.axis_size("zh")

    positions = jnp.arange(CAP, dtype=jnp.int32)
    selector = jnp.transpose(slot)[:, None, :] == positions[None, :, None]
    picked = selector.astype(jnp.bfloat16)
    rows_x = jnp.einsum("ect,td->ecd", picked, tokens, preferred_element_type=jnp.float32).astype(jnp.bfloat16)
    rows_dy = jnp.einsum("ect,td->ecd", picked, output_gradient, preferred_element_type=jnp.float32)
    gate = jnp.sum(jnp.where(selector, jnp.transpose(gate_weight)[:, None, :], 0.0), axis=2)
    rows_g = (rows_dy * gate[..., None]).astype(jnp.bfloat16)
    n_zl = lax.axis_size("zl")
    n_xc = n_half // n_zl
    rows = jnp.concatenate([rows_x, rows_g], axis=1).reshape(n_win, 2 * CAP, n_zl, n_xc, n_yl, LANE)
    rows = jnp.transpose(rows, (0, 4, 1, 3, 2, 5)).reshape(n_win, n_yl, 1, 2 * CAP, n_half * LANE)
    rows = jnp.broadcast_to(rows, (n_win, n_yl, n_zh, 2 * CAP, n_half * LANE))
    w_own = jnp.concatenate([gate_up_weight[0], jnp.transpose(down_weight[0])], axis=1)
    w_sent = jnp.broadcast_to(w_own.reshape(1, n_yl, LANE, 3 * hid), (n_zl, n_yl, LANE, 3 * hid))
    w_pair = a2a(w_sent.reshape(n_zl * n_yl, LANE, 3 * hid), ("zl", "yl"))
    rows, w_pair = lax.optimization_barrier((rows, w_pair))
    w_pair = w_pair.reshape(n_zl, n_yl, LANE, 3 * hid)
    w_mine = [w_pair[:, i, :, : 2 * hid] for i in range(n_yl)] + [w_pair[:, i, :, 2 * hid :] for i in range(n_yl)]
    w_mine = jnp.concatenate(w_mine, axis=2).reshape(n_zl * LANE, 3 * n_yl * hid)
    w_full = lax.all_gather(w_mine, ("x", "c"), axis=0, tiled=True)
    gu_cols = 2 * n_yl * hid
    w_gu, w_down = w_full[:, :gu_cols], w_full[:, gu_cols:]

    recv = a2a(rows.reshape(-1, 2 * CAP, n_half * LANE), EXPERT)
    n_src = recv.shape[0]
    x_mat = recv[:, :CAP].reshape(n_src * CAP, n_half * LANE)
    g_mat = recv[:, CAP:].reshape(n_src * CAP, n_half * LANE)

    part = jnp.concatenate(
        [f32_dot(x_mat, w_gu, ((1,), (0,))), f32_dot(g_mat, w_down, ((1,), (0,)))], axis=1
    ).astype(jnp.bfloat16)
    part_other, x_mat = lax.optimization_barrier((swap(part, "yl"), x_mat))
    total = part.astype(jnp.float32) + part_other.astype(jnp.float32)
    dgu = []
    for i in range(n_yl):
        pre, up = total[:, 2 * i * hid : (2 * i + 1) * hid], total[:, (2 * i + 1) * hid : (2 * i + 2) * hid]
        dh = total[:, gu_cols + i * hid : gu_cols + (i + 1) * hid]
        sig = jax.nn.sigmoid(pre)
        dgu += [dh * up * sig * (1.0 + pre * (1.0 - sig)), dh * (pre * sig)]
    dgu = jnp.concatenate(dgu, axis=1).astype(jnp.bfloat16)

    dx = f32_dot(dgu, w_gu, ((1,), (1,))).astype(jnp.bfloat16)
    dx, dgu = lax.optimization_barrier((dx, dgu))
    pgu = f32_dot(x_mat, dgu, ((0,), (0,))).astype(jnp.bfloat16)

    summed = lax.psum_scatter(pgu, ("x", "c"), scatter_dimension=0, tiled=True)
    summed = jnp.transpose(summed.reshape(n_zl, LANE, n_yl, 2 * hid), (0, 2, 1, 3))
    summed = a2a(summed.reshape(n_zl * n_yl, LANE, 2 * hid), ("zl", "yl"))
    grad_gu = jnp.sum(summed.reshape(n_zl, n_yl * LANE, 2 * hid).astype(jnp.float32), axis=0)
    grad_gu = grad_gu.astype(jnp.bfloat16)[None]

    back = a2a(dx.reshape(n_src, CAP, n_half * LANE), EXPERT)
    back = jnp.sum(back.reshape(n_win, n_yl, n_zh, CAP, n_xc, n_zl, LANE).astype(jnp.float32), axis=2)
    back = jnp.transpose(back, (0, 2, 4, 3, 1, 5)).reshape(n_win, CAP, width)
    grad_tokens = jnp.einsum("ect,ecd->td", selector.astype(jnp.float32), back).astype(jnp.bfloat16)
    return grad_tokens, grad_gu


def solution(mesh):
    fine = Mesh(mesh.devices.reshape(2, 4, 2, 4, 2, 4), FINE)
    dp, ex = FINE[:3], FINE[3:]
    in_specs = (P(FINE, None), P(FINE, None), P(FINE, None), P(FINE, None), P(ex, dp, None), P(ex, None, dp))
    out_specs = (P(FINE, None), P(ex, dp, None))
    return jax.shard_map(on_device, mesh=fine, in_specs=in_specs, out_specs=out_specs, check_vma=False)
```

```python
import jax
import jax.numpy as jnp
from jax import lax
from jax.experimental import pallas as pl
from jax.experimental.pallas import tpu as pltpu
from jax.sharding import Mesh, PartitionSpec as P

FINE = ("zl", "x", "c", "yh", "yl", "zh")
EXPERT = ("yh", "yl", "zh")
CAP = 8
LANE = 128


def f32_dot(a, b, dims):
    return lax.dot_general(a, b, (dims, ((), ())), preferred_element_type=jnp.float32)


def a2a(v, axes):
    return lax.all_to_all(v, axes, split_axis=0, concat_axis=0, tiled=True)


def swap(v, axis):
    return lax.ppermute(v, axis, [(0, 1), (1, 0)])


def split_kernel(core_ref, rows_ref, kept_ref, given_ref):
    n_src, _, depth = rows_ref.shape
    x = rows_ref[:, :CAP, :].reshape(n_src * CAP, depth)
    low, high = x[:, : depth // 2].T, x[:, depth // 2 :].T

    @pl.when(core_ref[0] == 0)
    def _():
        kept_ref[...], given_ref[...] = low, high

    @pl.when(core_ref[0] != 0)
    def _():
        kept_ref[...], given_ref[...] = high, low


def split_rows(core, recv, depth):
    n_src, rows, width = recv.shape
    out = jax.ShapeDtypeStruct((width // 2, n_src * CAP), recv.dtype)
    out_spec = pl.BlockSpec((depth // 2, n_src * CAP), lambda k: (k, 0))
    return pl.pallas_call(
        split_kernel,
        grid=(width // depth,),
        in_specs=[
            pl.BlockSpec(memory_space=pltpu.SMEM),
            pl.BlockSpec((n_src, rows, depth), lambda k: (0, 0, k)),
        ],
        out_specs=[out_spec, out_spec],
        out_shape=[out, out],
        name="split_rows",
    )(core.reshape(1), recv)


def pack_kernel(gu_ref, down_ref, out_ref):
    n_zl, n_yl, _, lanes = out_ref.shape
    gu_cols = gu_ref.shape[1]
    for j in range(n_yl):
        half = slice(j * lanes, (j + 1) * lanes)
        gu_t = gu_ref[half, :].T
        for i in range(n_zl):
            out_ref[i, j, :gu_cols, :] = gu_t
            out_ref[i, j, gu_cols:, :] = down_ref[:, half]


def pack_weights(gate_up, down, n_zl, n_yl):
    shape = (n_zl, n_yl, gate_up.shape[1] + down.shape[0], LANE)
    out = pl.pallas_call(pack_kernel, out_shape=jax.ShapeDtypeStruct(shape, gate_up.dtype), name="pack_weights")(
        gate_up, down
    )
    return out.reshape(n_zl * n_yl, shape[2], LANE)


def order_kernel(pair_ref, out_ref):
    n_zl, n_yl, units, lanes = pair_ref.shape
    gu_cols = 2 * units // 3
    for i in range(n_zl):
        pair = [pair_ref[i, j] for j in range(n_yl)]
        turned = jnp.concatenate([p[:gu_cols] for p in pair] + [p[gu_cols:] for p in pair], axis=0).T
        out_ref[i * lanes : (i + 1) * lanes, :] = turned


def order_weights(pair, n_zl, n_yl):
    _, units, lanes = pair.shape
    out = jax.ShapeDtypeStruct((n_zl * lanes, n_yl * units), pair.dtype)
    return pl.pallas_call(order_kernel, out_shape=out, name="order_weights")(pair.reshape(n_zl, n_yl, units, lanes))


def on_device(tokens, output_gradient, slot, gate_weight, gate_up_weight, down_weight):
    n_win = slot.shape[1]
    width = tokens.shape[1]
    n_half = width // (2 * LANE)
    hid = down_weight.shape[1]
    n_yl, n_zh, n_c = lax.axis_size("yl"), lax.axis_size("zh"), lax.axis_size("c")

    positions = jnp.arange(CAP, dtype=jnp.int32)
    selector = jnp.transpose(slot)[:, None, :] == positions[None, :, None]
    picked = selector.astype(jnp.bfloat16)
    rows_x = jnp.einsum("ect,td->ecd", picked, tokens, preferred_element_type=jnp.float32).astype(jnp.bfloat16)
    rows_dy = jnp.einsum("ect,td->ecd", picked, output_gradient, preferred_element_type=jnp.float32)
    gate = jnp.sum(jnp.where(selector, jnp.transpose(gate_weight)[:, None, :], 0.0), axis=2)
    rows_g = (rows_dy * gate[..., None]).astype(jnp.bfloat16)
    n_zl = lax.axis_size("zl")
    n_xc = n_half // n_zl
    rows = jnp.concatenate([rows_x, rows_g], axis=1).reshape(n_win, 2 * CAP, n_zl, n_xc, n_yl, LANE)
    rows = jnp.transpose(rows, (0, 4, 1, 3, 2, 5)).reshape(n_win, n_yl, 1, 2 * CAP, n_half * LANE)
    rows = jnp.broadcast_to(rows, (n_win, n_yl, n_zh, 2 * CAP, n_half * LANE))
    rows = rows.reshape(-1, 2 * CAP, n_half * LANE)

    w_pair = a2a(pack_weights(gate_up_weight[0], down_weight[0], n_zl, n_yl), ("zl", "yl"))
    rows, w_pair = lax.optimization_barrier((rows, w_pair))
    w_full = lax.all_gather(order_weights(w_pair, n_zl, n_yl), ("x", "c"), axis=0, tiled=True)
    gu_cols = 2 * n_yl * hid
    w_gu, w_down = w_full[:, :gu_cols], w_full[:, gu_cols:]

    recv = a2a(rows, EXPERT)
    n_src = recv.shape[0]
    x_mat = recv[:, :CAP].reshape(n_src * CAP, n_half * LANE)
    g_mat = recv[:, CAP:].reshape(n_src * CAP, n_half * LANE)

    part = jnp.concatenate(
        [f32_dot(x_mat, w_gu, ((1,), (0,))), f32_dot(g_mat, w_down, ((1,), (0,)))], axis=1
    ).astype(jnp.bfloat16)

    part, recv = lax.optimization_barrier((part, recv))
    xt_kept, xt_given = split_rows(lax.axis_index("c"), recv, n_c * n_zl * LANE)
    part_other, xt_kept, xt_got = lax.optimization_barrier((swap(part, "yl"), xt_kept, swap(xt_given, "c")))

    total = part.astype(jnp.float32) + part_other.astype(jnp.float32)
    dgu = []
    for i in range(n_yl):
        pre, up = total[:, 2 * i * hid : (2 * i + 1) * hid], total[:, (2 * i + 1) * hid : (2 * i + 2) * hid]
        dh = total[:, gu_cols + i * hid : gu_cols + (i + 1) * hid]
        sig = jax.nn.sigmoid(pre)
        dgu += [dh * up * sig * (1.0 + pre * (1.0 - sig)), dh * (pre * sig)]
    dgu = jnp.concatenate(dgu, axis=1).astype(jnp.bfloat16)

    dx = f32_dot(dgu, w_gu, ((1,), (1,))).astype(jnp.bfloat16)
    dx, dgu_other = lax.optimization_barrier((dx, swap(dgu, "c")))
    both = jnp.concatenate([dgu, dgu_other], axis=0)
    pgu = jnp.dot(jnp.concatenate([xt_kept, xt_got], axis=1), both, preferred_element_type=jnp.float32).astype(jnp.bfloat16)

    summed = lax.psum_scatter(pgu, "x", scatter_dimension=0, tiled=True)
    summed = jnp.transpose(summed.reshape(n_zl, LANE, n_yl, 2 * hid), (0, 2, 1, 3))
    summed = a2a(summed.reshape(n_zl * n_yl, LANE, 2 * hid), ("zl", "yl"))
    grad_gu = jnp.sum(summed.reshape(n_zl, n_yl * LANE, 2 * hid).astype(jnp.float32), axis=0)
    grad_gu = grad_gu.astype(jnp.bfloat16)[None]

    back = a2a(dx.reshape(n_src, CAP, n_half * LANE), EXPERT)
    back = jnp.sum(back.reshape(n_win, n_yl, n_zh, CAP, n_xc, n_zl, LANE).astype(jnp.float32), axis=2)
    back = jnp.transpose(back, (0, 2, 4, 3, 1, 5)).reshape(n_win, CAP, width)
    grad_tokens = jnp.einsum("ect,ecd->td", selector.astype(jnp.float32), back).astype(jnp.bfloat16)
    return grad_tokens, grad_gu


def solution(mesh):
    fine = Mesh(mesh.devices.reshape(2, 4, 2, 4, 2, 4), FINE)
    dp, ex = FINE[:3], FINE[3:]
    in_specs = (P(FINE, None), P(FINE, None), P(FINE, None), P(FINE, None), P(ex, dp, None), P(ex, None, dp))
    out_specs = (P(FINE, None), P(ex, dp, None))
    return jax.shard_map(on_device, mesh=fine, in_specs=in_specs, out_specs=out_specs, check_vma=False)
```

```python
import jax
import jax.numpy as jnp
from jax import lax
from jax.experimental import pallas as pl
from jax.experimental.pallas import tpu as pltpu
from jax.sharding import Mesh, PartitionSpec as P

FINE = ("zl", "x", "c", "yh", "yl", "zh")
EXPERT = ("yh", "yl", "zh")
CAP = 8
LANE = 128


def f32_dot(a, b, dims):
    return lax.dot_general(a, b, (dims, ((), ())), preferred_element_type=jnp.float32)


def a2a(v, axes):
    return lax.all_to_all(v, axes, split_axis=0, concat_axis=0, tiled=True)


def swap(v, axis):
    return lax.ppermute(v, axis, [(0, 1), (1, 0)])


def split_kernel(core_ref, rows_ref, kept_ref, given_ref):
    n_src, _, depth = rows_ref.shape
    x = rows_ref[:, :CAP, :].reshape(n_src * CAP, depth)
    low, high = x[:, : depth // 2].T, x[:, depth // 2 :].T

    @pl.when(core_ref[0] == 0)
    def _():
        kept_ref[...], given_ref[...] = low, high

    @pl.when(core_ref[0] != 0)
    def _():
        kept_ref[...], given_ref[...] = high, low


def split_rows(core, recv, depth):
    n_src, rows, width = recv.shape
    out = jax.ShapeDtypeStruct((width // 2, n_src * CAP), recv.dtype)
    out_spec = pl.BlockSpec((depth // 2, n_src * CAP), lambda k: (k, 0))
    return pl.pallas_call(
        split_kernel,
        grid=(width // depth,),
        in_specs=[
            pl.BlockSpec(memory_space=pltpu.SMEM),
            pl.BlockSpec((n_src, rows, depth), lambda k: (0, 0, k)),
        ],
        out_specs=[out_spec, out_spec],
        out_shape=[out, out],
        name="split_rows",
    )(core.reshape(1), recv)


def pack_kernel(gu_ref, down_ref, out_ref):
    n_zl, n_yl, _, lanes = out_ref.shape
    gu_cols = gu_ref.shape[1]
    for j in range(n_yl):
        half = slice(j * lanes, (j + 1) * lanes)
        gu_t = gu_ref[half, :].T
        for i in range(n_zl):
            out_ref[i, j, :gu_cols, :] = gu_t
            out_ref[i, j, gu_cols:, :] = down_ref[:, half]


def pack_weights(gate_up, down, n_zl, n_yl):
    shape = (n_zl, n_yl, gate_up.shape[1] + down.shape[0], LANE)
    out = pl.pallas_call(pack_kernel, out_shape=jax.ShapeDtypeStruct(shape, gate_up.dtype), name="pack_weights")(
        gate_up, down
    )
    return out.reshape(n_zl * n_yl, shape[2], LANE)


def on_device(tokens, output_gradient, slot, gate_weight, gate_up_weight, down_weight):
    n_win = slot.shape[1]
    width = tokens.shape[1]
    n_half = width // (2 * LANE)
    hid = down_weight.shape[1]
    n_yl, n_zh, n_c = lax.axis_size("yl"), lax.axis_size("zh"), lax.axis_size("c")

    positions = jnp.arange(CAP, dtype=jnp.int32)
    selector = jnp.transpose(slot)[:, None, :] == positions[None, :, None]
    picked = selector.astype(jnp.bfloat16)
    rows_x = jnp.einsum("ect,td->ecd", picked, tokens, preferred_element_type=jnp.float32).astype(jnp.bfloat16)
    rows_dy = jnp.einsum("ect,td->ecd", picked, output_gradient, preferred_element_type=jnp.float32)
    gate = jnp.sum(jnp.where(selector, jnp.transpose(gate_weight)[:, None, :], 0.0), axis=2)
    rows_g = (rows_dy * gate[..., None]).astype(jnp.bfloat16)
    n_zl = lax.axis_size("zl")
    n_xc = n_half // n_zl
    rows = jnp.concatenate([rows_x, rows_g], axis=1).reshape(n_win, 2 * CAP, n_zl, n_xc, n_yl, LANE)
    rows = jnp.transpose(rows, (0, 4, 1, 3, 2, 5)).reshape(n_win, n_yl, 1, 2 * CAP, n_half * LANE)
    rows = jnp.broadcast_to(rows, (n_win, n_yl, n_zh, 2 * CAP, n_half * LANE))
    rows = rows.reshape(-1, 2 * CAP, n_half * LANE)

    w_pair = a2a(pack_weights(gate_up_weight[0], down_weight[0], n_zl, n_yl), ("zl", "yl"))
    rows, w_pair = lax.optimization_barrier((rows, w_pair))
    w_all = lax.all_gather(w_pair.reshape(-1, LANE), ("x", "c"), axis=0, tiled=True)
    w_all = w_all.reshape(n_xc, n_zl, n_yl, 3 * hid, LANE)
    gu_cols = 2 * n_yl * hid
    w_gu_t = jnp.transpose(w_all[:, :, :, : 2 * hid], (2, 3, 0, 1, 4)).reshape(gu_cols, n_half * LANE)
    w_down_t = jnp.transpose(w_all[:, :, :, 2 * hid :], (2, 3, 0, 1, 4)).reshape(n_yl * hid, n_half * LANE)
    recv, w_gu_t, w_down_t = lax.optimization_barrier((a2a(rows, EXPERT), w_gu_t, w_down_t))
    n_src = recv.shape[0]
    x_mat = recv[:, :CAP].reshape(n_src * CAP, n_half * LANE)
    g_mat = recv[:, CAP:].reshape(n_src * CAP, n_half * LANE)

    part = jnp.concatenate(
        [f32_dot(x_mat, w_gu_t, ((1,), (1,))), f32_dot(g_mat, w_down_t, ((1,), (1,)))], axis=1
    ).astype(jnp.bfloat16)

    part, recv = lax.optimization_barrier((part, recv))
    xt_kept, xt_given = split_rows(lax.axis_index("c"), recv, n_c * n_zl * LANE)
    part_other, xt_kept, xt_got = lax.optimization_barrier((swap(part, "yl"), xt_kept, swap(xt_given, "c")))

    total = part.astype(jnp.float32) + part_other.astype(jnp.float32)
    dgu = []
    for i in range(n_yl):
        pre, up = total[:, 2 * i * hid : (2 * i + 1) * hid], total[:, (2 * i + 1) * hid : (2 * i + 2) * hid]
        dh = total[:, gu_cols + i * hid : gu_cols + (i + 1) * hid]
        sig = jax.nn.sigmoid(pre)
        dgu += [dh * up * sig * (1.0 + pre * (1.0 - sig)), dh * (pre * sig)]
    dgu = jnp.concatenate(dgu, axis=1).astype(jnp.bfloat16)

    dx = jnp.dot(dgu, w_gu_t, preferred_element_type=jnp.float32).astype(jnp.bfloat16)
    dx, dgu_other = lax.optimization_barrier((dx, swap(dgu, "c")))
    both = jnp.concatenate([dgu, dgu_other], axis=0)
    pgu = jnp.dot(jnp.concatenate([xt_kept, xt_got], axis=1), both, preferred_element_type=jnp.float32).astype(jnp.bfloat16)

    summed = lax.psum_scatter(pgu, "x", scatter_dimension=0, tiled=True)
    zl, yl = lax.axis_index("zl"), lax.axis_index("yl")

    def block(zl_to, yl_to):
        return lax.dynamic_slice(summed, (zl_to * LANE, yl_to * 2 * hid), (LANE, 2 * hid))

    def flipped(v, flip):
        return lax.ppermute(v, ("zl", "yl"), [(i, i ^ flip) for i in range(n_zl * n_yl)])

    mine, other = block(zl, yl), flipped(block(zl, 1 - yl), 1)
    mine2, other2 = flipped(block(1 - zl, yl), 2), flipped(block(1 - zl, 1 - yl), 3)
    back = a2a(dx.reshape(n_src, CAP, n_half * LANE), EXPERT)
    back, other, mine2, other2 = lax.optimization_barrier((back, other, mine2, other2))
    mine = (mine.astype(jnp.float32) + mine2.astype(jnp.float32)).astype(jnp.bfloat16)
    other = (other.astype(jnp.float32) + other2.astype(jnp.float32)).astype(jnp.bfloat16)
    low, high = jnp.where(yl == 0, mine, other), jnp.where(yl == 0, other, mine)
    grad_gu = jnp.concatenate([low, high], axis=0)[None]

    back = jnp.sum(back.reshape(n_win, n_yl, n_zh, CAP, n_xc, n_zl, LANE).astype(jnp.float32), axis=2)
    back = jnp.transpose(back, (0, 2, 4, 3, 1, 5)).reshape(n_win, CAP, width)
    grad_tokens = jnp.einsum("ect,ecd->td", selector.astype(jnp.float32), back).astype(jnp.bfloat16)
    return grad_tokens, grad_gu


def solution(mesh):
    fine = Mesh(mesh.devices.reshape(2, 4, 2, 4, 2, 4), FINE)
    dp, ex = FINE[:3], FINE[3:]
    in_specs = (P(FINE, None), P(FINE, None), P(FINE, None), P(FINE, None), P(ex, dp, None), P(ex, None, dp))
    out_specs = (P(FINE, None), P(ex, dp, None))
    return jax.shard_map(on_device, mesh=fine, in_specs=in_specs, out_specs=out_specs, check_vma=False)
```

```python
import jax
import jax.numpy as jnp
from jax import lax
from jax.experimental import pallas as pl
from jax.experimental.pallas import tpu as pltpu
from jax.sharding import Mesh, PartitionSpec as P

FINE = ("zl", "x", "c", "yh", "yl", "zh")
EXPERT = ("yh", "yl", "zh")
CAP = 8
LANE = 128


def f32_dot(a, b, dims):
    return lax.dot_general(a, b, (dims, ((), ())), preferred_element_type=jnp.float32)


def a2a(v, axes):
    return lax.all_to_all(v, axes, split_axis=0, concat_axis=0, tiled=True)


def swap(v, axis):
    return lax.ppermute(v, axis, [(0, 1), (1, 0)])


def split_kernel(core_ref, rows_ref, kept_ref, given_ref):
    n_src, _, depth = rows_ref.shape
    x = rows_ref[:, :CAP, :].reshape(n_src * CAP, depth)
    low, high = x[:, : depth // 2].T, x[:, depth // 2 :].T

    @pl.when(core_ref[0] == 0)
    def _():
        kept_ref[...], given_ref[...] = low, high

    @pl.when(core_ref[0] != 0)
    def _():
        kept_ref[...], given_ref[...] = high, low


def split_rows(core, recv, depth):
    n_src, rows, width = recv.shape
    out = jax.ShapeDtypeStruct((width // 2, n_src * CAP), recv.dtype)
    out_spec = pl.BlockSpec((depth // 2, n_src * CAP), lambda k: (k, 0))
    return pl.pallas_call(
        split_kernel,
        grid=(width // depth,),
        in_specs=[
            pl.BlockSpec(memory_space=pltpu.SMEM),
            pl.BlockSpec((n_src, rows, depth), lambda k: (0, 0, k)),
        ],
        out_specs=[out_spec, out_spec],
        out_shape=[out, out],
        name="split_rows",
    )(core.reshape(1), recv)


def pack_kernel(gu_ref, down_ref, out_ref):
    n_zl, n_yl, _, lanes = out_ref.shape
    gu_cols = gu_ref.shape[1]
    for j in range(n_yl):
        half = slice(j * lanes, (j + 1) * lanes)
        gu_t = gu_ref[half, :].T
        for i in range(n_zl):
            out_ref[i, j, :gu_cols, :] = gu_t
            out_ref[i, j, gu_cols:, :] = down_ref[:, half]


def pack_weights(gate_up, down, n_zl, n_yl):
    shape = (n_zl, n_yl, gate_up.shape[1] + down.shape[0], LANE)
    out = pl.pallas_call(pack_kernel, out_shape=jax.ShapeDtypeStruct(shape, gate_up.dtype), name="pack_weights")(
        gate_up, down
    )
    return out.reshape(n_zl * n_yl, shape[2], LANE)


def order_kernel(w_ref, gu_ref, down_ref):
    n_zl, n_yl, units, lanes = w_ref.shape
    hid = units // 3
    for i in range(n_zl):
        cols = slice(i * lanes, (i + 1) * lanes)
        for j in range(n_yl):
            gu_ref[2 * j * hid : 2 * (j + 1) * hid, cols] = w_ref[i, j, : 2 * hid, :]
            down_ref[j * hid : (j + 1) * hid, cols] = w_ref[i, j, 2 * hid :, :]


def order_weights(w_all):
    n_xc, n_zl, n_yl, units, lanes = w_all.shape
    hid = units // 3
    gu_rows, down_rows, cols = 2 * hid * n_yl, hid * n_yl, n_zl * lanes
    return pl.pallas_call(
        order_kernel,
        grid=(n_xc,),
        in_specs=[pl.BlockSpec((None, n_zl, n_yl, units, lanes), lambda k: (k, 0, 0, 0, 0))],
        out_specs=[pl.BlockSpec((gu_rows, cols), lambda k: (0, k)), pl.BlockSpec((down_rows, cols), lambda k: (0, k))],
        out_shape=[
            jax.ShapeDtypeStruct((gu_rows, n_xc * cols), w_all.dtype),
            jax.ShapeDtypeStruct((down_rows, n_xc * cols), w_all.dtype),
        ],
        name="order_weights",
    )(w_all)


def rows_kernel(n_zl, tokens_ref, dy_ref, slot_ref, gate_ref, out_ref):
    n_win, n_yl, n_zh, _, half = out_ref.shape
    n_tok = tokens_ref.shape[0]
    n_xc = half // (n_zl * LANE)
    positions = lax.broadcasted_iota(jnp.int32, (CAP, n_tok), 0)
    for e in range(n_win):
        picked = jnp.broadcast_to(slot_ref[e : e + 1, :], (CAP, n_tok)) == positions
        gate = jnp.sum(jnp.where(picked, gate_ref[e : e + 1, :], 0.0), axis=1, keepdims=True)
        one_hot = picked.astype(jnp.float32).astype(tokens_ref.dtype)
        x = jnp.dot(one_hot, tokens_ref[...], preferred_element_type=jnp.float32)
        g = jnp.dot(one_hot, dy_ref[...], preferred_element_type=jnp.float32) * gate
        both = jnp.concatenate([x, g], axis=0).astype(out_ref.dtype)
        for h in range(n_yl):
            for xc in range(n_xc):
                for zl in range(n_zl):
                    src = ((zl * n_xc + xc) * n_yl + h) * LANE
                    dst = (xc * n_zl + zl) * LANE
                    piece = both[:, src : src + LANE]
                    for zh in range(n_zh):
                        out_ref[e, h, zh, :, dst : dst + LANE] = piece


def select_rows(tokens, dy, slot_t, gate_t, n_zl, n_yl, n_zh):
    n_win, width = slot_t.shape[0], tokens.shape[1]
    shape = (n_win, n_yl, n_zh, 2 * CAP, width // n_yl)
    return pl.pallas_call(
        lambda *refs: rows_kernel(n_zl, *refs), out_shape=jax.ShapeDtypeStruct(shape, tokens.dtype), name="select_rows"
    )(tokens, dy, slot_t, gate_t)


def on_device(tokens, output_gradient, slot, gate_weight, gate_up_weight, down_weight):
    n_win = slot.shape[1]
    width = tokens.shape[1]
    n_half = width // (2 * LANE)
    hid = down_weight.shape[1]
    n_yl, n_zh, n_c = lax.axis_size("yl"), lax.axis_size("zh"), lax.axis_size("c")

    n_zl = lax.axis_size("zl")
    n_xc = n_half // n_zl
    rows = select_rows(tokens, output_gradient, jnp.transpose(slot), jnp.transpose(gate_weight), n_zl, n_yl, n_zh)
    rows = rows.reshape(-1, 2 * CAP, n_half * LANE)

    w_pair = a2a(pack_weights(gate_up_weight[0], down_weight[0], n_zl, n_yl), ("zl", "yl"))
    rows, w_pair = lax.optimization_barrier((rows, w_pair))
    w_all = lax.all_gather(w_pair.reshape(-1, LANE), ("x", "c"), axis=0, tiled=True)
    w_all = w_all.reshape(n_xc, n_zl, n_yl, 3 * hid, LANE)
    gu_cols = 2 * n_yl * hid
    w_gu_t, w_down_t = order_weights(w_all)
    recv, w_gu_t, w_down_t = lax.optimization_barrier((a2a(rows, EXPERT), w_gu_t, w_down_t))
    n_src = recv.shape[0]
    x_mat = recv[:, :CAP].reshape(n_src * CAP, n_half * LANE)
    g_mat = recv[:, CAP:].reshape(n_src * CAP, n_half * LANE)

    part = jnp.concatenate(
        [f32_dot(x_mat, w_gu_t, ((1,), (1,))), f32_dot(g_mat, w_down_t, ((1,), (1,)))], axis=1
    ).astype(jnp.bfloat16)

    part, recv = lax.optimization_barrier((part, recv))
    xt_kept, xt_given = split_rows(lax.axis_index("c"), recv, n_c * n_zl * LANE)
    part_other, xt_kept, xt_got = lax.optimization_barrier((swap(part, "yl"), xt_kept, swap(xt_given, "c")))

    total = part.astype(jnp.float32) + part_other.astype(jnp.float32)
    dgu = []
    for i in range(n_yl):
        pre, up = total[:, 2 * i * hid : (2 * i + 1) * hid], total[:, (2 * i + 1) * hid : (2 * i + 2) * hid]
        dh = total[:, gu_cols + i * hid : gu_cols + (i + 1) * hid]
        sig = jax.nn.sigmoid(pre)
        dgu += [dh * up * sig * (1.0 + pre * (1.0 - sig)), dh * (pre * sig)]
    dgu = jnp.concatenate(dgu, axis=1).astype(jnp.bfloat16)

    dx = jnp.dot(dgu, w_gu_t, preferred_element_type=jnp.float32).astype(jnp.bfloat16)
    dx, dgu_other = lax.optimization_barrier((dx, swap(dgu, "c")))
    both = jnp.concatenate([dgu, dgu_other], axis=0)
    pgu = jnp.dot(jnp.concatenate([xt_kept, xt_got], axis=1), both, preferred_element_type=jnp.float32).astype(jnp.bfloat16)

    summed = lax.psum_scatter(pgu, "x", scatter_dimension=0, tiled=True)
    zl, yl = lax.axis_index("zl"), lax.axis_index("yl")

    def block(zl_to, yl_to):
        return lax.dynamic_slice(summed, (zl_to * LANE, yl_to * 2 * hid), (LANE, 2 * hid))

    def flipped(v, flip):
        return lax.ppermute(v, ("zl", "yl"), [(i, i ^ flip) for i in range(n_zl * n_yl)])

    mine, other = block(zl, yl), flipped(block(zl, 1 - yl), 1)
    mine2, other2 = flipped(block(1 - zl, yl), 2), flipped(block(1 - zl, 1 - yl), 3)
    back = a2a(dx.reshape(n_src, CAP, n_half * LANE), EXPERT)
    back, other, mine2, other2 = lax.optimization_barrier((back, other, mine2, other2))
    mine = (mine.astype(jnp.float32) + mine2.astype(jnp.float32)).astype(jnp.bfloat16)
    other = (other.astype(jnp.float32) + other2.astype(jnp.float32)).astype(jnp.bfloat16)
    low, high = jnp.where(yl == 0, mine, other), jnp.where(yl == 0, other, mine)
    grad_gu = jnp.concatenate([low, high], axis=0)[None]

    back = jnp.sum(back.reshape(n_win, n_yl, n_zh, CAP, n_xc, n_zl, LANE).astype(jnp.float32), axis=2)
    back = jnp.transpose(back, (0, 2, 4, 3, 1, 5)).reshape(n_win, CAP, width)
    positions = jnp.arange(CAP, dtype=jnp.int32)
    selector = jnp.transpose(slot)[:, None, :] == positions[None, :, None]
    grad_tokens = jnp.einsum("ect,ecd->td", selector.astype(jnp.float32), back).astype(jnp.bfloat16)
    return grad_tokens, grad_gu


def solution(mesh):
    fine = Mesh(mesh.devices.reshape(2, 4, 2, 4, 2, 4), FINE)
    dp, ex = FINE[:3], FINE[3:]
    in_specs = (P(FINE, None), P(FINE, None), P(FINE, None), P(FINE, None), P(ex, dp, None), P(ex, None, dp))
    out_specs = (P(FINE, None), P(ex, dp, None))
    return jax.shard_map(on_device, mesh=fine, in_specs=in_specs, out_specs=out_specs, check_vma=False)
```

```python
import jax
import jax.numpy as jnp
from jax import lax
from jax.experimental import pallas as pl
from jax.sharding import Mesh, PartitionSpec as P

FINE = ("zl", "x", "c", "yh", "yl", "zh")
EXPERT = ("yh", "yl", "zh")
CAP = 8
LANE = 128


def f32_dot(a, b, dims):
    return lax.dot_general(a, b, (dims, ((), ())), preferred_element_type=jnp.float32)


def a2a(v, axes):
    return lax.all_to_all(v, axes, split_axis=0, concat_axis=0, tiled=True)


def swap(v, axis):
    return lax.ppermute(v, axis, [(0, 1), (1, 0)])


def pack_kernel(gu_ref, down_ref, out_ref):
    n_zl, n_yl, _, lanes = out_ref.shape
    gu_cols = gu_ref.shape[1]
    for j in range(n_yl):
        half = slice(j * lanes, (j + 1) * lanes)
        gu_t = gu_ref[half, :].T
        for i in range(n_zl):
            out_ref[i, j, :gu_cols, :] = gu_t
            out_ref[i, j, gu_cols:, :] = down_ref[:, half]


def pack_weights(gate_up, down, n_zl, n_yl):
    shape = (n_zl, n_yl, gate_up.shape[1] + down.shape[0], LANE)
    out = pl.pallas_call(pack_kernel, out_shape=jax.ShapeDtypeStruct(shape, gate_up.dtype), name="pack_weights")(
        gate_up, down
    )
    return out.reshape(n_zl * n_yl, shape[2], LANE)


def order_kernel(w_ref, gu_ref, down_ref):
    n_zl, n_yl, units, lanes = w_ref.shape
    hid = units // 3
    for i in range(n_zl):
        cols = slice(i * lanes, (i + 1) * lanes)
        for j in range(n_yl):
            gu_ref[2 * j * hid : 2 * (j + 1) * hid, cols] = w_ref[i, j, : 2 * hid, :]
            down_ref[j * hid : (j + 1) * hid, cols] = w_ref[i, j, 2 * hid :, :]


def order_weights(w_all):
    n_xc, n_zl, n_yl, units, lanes = w_all.shape
    hid = units // 3
    gu_rows, down_rows, cols = 2 * hid * n_yl, hid * n_yl, n_zl * lanes
    return pl.pallas_call(
        order_kernel,
        grid=(n_xc,),
        in_specs=[pl.BlockSpec((None, n_zl, n_yl, units, lanes), lambda k: (k, 0, 0, 0, 0))],
        out_specs=[pl.BlockSpec((gu_rows, cols), lambda k: (0, k)), pl.BlockSpec((down_rows, cols), lambda k: (0, k))],
        out_shape=[
            jax.ShapeDtypeStruct((gu_rows, n_xc * cols), w_all.dtype),
            jax.ShapeDtypeStruct((down_rows, n_xc * cols), w_all.dtype),
        ],
        name="order_weights",
    )(w_all)


def rows_kernel(n_zl, tokens_ref, dy_ref, slot_ref, gate_ref, out_ref):
    n_win, n_yl, n_zh, _, half = out_ref.shape
    n_tok = tokens_ref.shape[0]
    n_xc = half // (n_zl * LANE)
    positions = lax.broadcasted_iota(jnp.int32, (CAP, n_tok), 0)
    for e in range(n_win):
        picked = jnp.broadcast_to(slot_ref[e : e + 1, :], (CAP, n_tok)) == positions
        gate = jnp.sum(jnp.where(picked, gate_ref[e : e + 1, :], 0.0), axis=1, keepdims=True)
        one_hot = picked.astype(jnp.float32).astype(tokens_ref.dtype)
        x = jnp.dot(one_hot, tokens_ref[...], preferred_element_type=jnp.float32)
        g = jnp.dot(one_hot, dy_ref[...], preferred_element_type=jnp.float32) * gate
        both = jnp.concatenate([x, g], axis=0).astype(out_ref.dtype)
        for h in range(n_yl):
            for xc in range(n_xc):
                for zl in range(n_zl):
                    src = ((zl * n_xc + xc) * n_yl + h) * LANE
                    dst = (xc * n_zl + zl) * LANE
                    piece = both[:, src : src + LANE]
                    for zh in range(n_zh):
                        out_ref[e, h, zh, :, dst : dst + LANE] = piece


def select_rows(tokens, dy, slot_t, gate_t, n_zl, n_yl, n_zh):
    n_win, width = slot_t.shape[0], tokens.shape[1]
    shape = (n_win, n_yl, n_zh, 2 * CAP, width // n_yl)
    return pl.pallas_call(
        lambda *refs: rows_kernel(n_zl, *refs), out_shape=jax.ShapeDtypeStruct(shape, tokens.dtype), name="select_rows"
    )(tokens, dy, slot_t, gate_t)


def on_device(tokens, output_gradient, slot, gate_weight, gate_up_weight, down_weight):
    n_win = slot.shape[1]
    width = tokens.shape[1]
    n_half = width // (2 * LANE)
    hid = down_weight.shape[1]
    n_yl, n_zh = lax.axis_size("yl"), lax.axis_size("zh")

    n_zl = lax.axis_size("zl")
    n_xc = n_half // n_zl
    rows = select_rows(tokens, output_gradient, jnp.transpose(slot), jnp.transpose(gate_weight), n_zl, n_yl, n_zh)
    rows = rows.reshape(-1, 2 * CAP, n_half * LANE)

    w_pair = a2a(pack_weights(gate_up_weight[0], down_weight[0], n_zl, n_yl), ("zl", "yl"))
    rows, w_pair = lax.optimization_barrier((rows, w_pair))
    w_all = lax.all_gather(w_pair.reshape(-1, LANE), ("x", "c"), axis=0, tiled=True)
    w_all = w_all.reshape(n_xc, n_zl, n_yl, 3 * hid, LANE)
    gu_cols = 2 * n_yl * hid
    w_gu_t, w_down_t = order_weights(w_all)
    recv, w_gu_t, w_down_t = lax.optimization_barrier((a2a(rows, EXPERT), w_gu_t, w_down_t))
    n_src = recv.shape[0]
    x_mat = recv[:, :CAP].reshape(n_src * CAP, n_half * LANE)
    g_mat = recv[:, CAP:].reshape(n_src * CAP, n_half * LANE)

    part = jnp.concatenate(
        [f32_dot(x_mat, w_gu_t, ((1,), (1,))), f32_dot(g_mat, w_down_t, ((1,), (1,)))], axis=1
    ).astype(jnp.bfloat16)

    total = part.astype(jnp.float32) + swap(part, "yl").astype(jnp.float32)
    dgu = []
    for i in range(n_yl):
        pre, up = total[:, 2 * i * hid : (2 * i + 1) * hid], total[:, (2 * i + 1) * hid : (2 * i + 2) * hid]
        dh = total[:, gu_cols + i * hid : gu_cols + (i + 1) * hid]
        sig = jax.nn.sigmoid(pre)
        dgu += [dh * up * sig * (1.0 + pre * (1.0 - sig)), dh * (pre * sig)]
    dgu = jnp.concatenate(dgu, axis=1).astype(jnp.bfloat16)

    pgu = f32_dot(x_mat, dgu, ((0,), (0,))).astype(jnp.bfloat16)
    dx = jnp.dot(dgu, w_gu_t, preferred_element_type=jnp.float32).astype(jnp.bfloat16)

    summed = lax.psum_scatter(pgu, ("x", "c"), scatter_dimension=0, tiled=True)
    summed = jnp.transpose(summed.reshape(n_zl, LANE, n_yl, 2 * hid), (0, 2, 1, 3))
    summed = a2a(summed.reshape(n_zl * n_yl, LANE, 2 * hid), ("zl", "yl"))
    grad_gu = jnp.sum(summed.reshape(n_zl, n_yl * LANE, 2 * hid).astype(jnp.float32), axis=0)
    grad_gu = grad_gu.astype(jnp.bfloat16)[None]

    back = a2a(dx.reshape(n_src, CAP, n_half * LANE), EXPERT)
    back = jnp.sum(back.reshape(n_win, n_yl, n_zh, CAP, n_xc, n_zl, LANE).astype(jnp.float32), axis=2)
    back = jnp.transpose(back, (0, 2, 4, 3, 1, 5)).reshape(n_win, CAP, width)
    positions = jnp.arange(CAP, dtype=jnp.int32)
    selector = jnp.transpose(slot)[:, None, :] == positions[None, :, None]
    grad_tokens = jnp.einsum("ect,ecd->td", selector.astype(jnp.float32), back).astype(jnp.bfloat16)
    return grad_tokens, grad_gu


def solution(mesh):
    fine = Mesh(mesh.devices.reshape(2, 4, 2, 4, 2, 4), FINE)
    dp, ex = FINE[:3], FINE[3:]
    in_specs = (P(FINE, None), P(FINE, None), P(FINE, None), P(FINE, None), P(ex, dp, None), P(ex, None, dp))
    out_specs = (P(FINE, None), P(ex, dp, None))
    return jax.shard_map(on_device, mesh=fine, in_specs=in_specs, out_specs=out_specs, check_vma=False)
```

```python
import jax
import jax.numpy as jnp
from jax import lax
from jax.experimental import pallas as pl
from jax.experimental.pallas import tpu as pltpu
from jax.sharding import Mesh, PartitionSpec as P

FINE = ("zl", "x", "c", "yh", "yl", "zh")
EXPERT = ("yh", "yl", "zh")
CAP = 8
LANE = 128


def f32_dot(a, b, dims):
    return lax.dot_general(a, b, (dims, ((), ())), preferred_element_type=jnp.float32)


def a2a(v, axes):
    return lax.all_to_all(v, axes, split_axis=0, concat_axis=0, tiled=True)


def swap(v, axis):
    return lax.ppermute(v, axis, [(0, 1), (1, 0)])


def split_kernel(core_ref, rows_ref, kept_ref, given_ref):
    n_src, _, depth = rows_ref.shape
    x = rows_ref[:, :CAP, :].reshape(n_src * CAP, depth)
    low, high = x[:, : depth // 2].T, x[:, depth // 2 :].T

    @pl.when(core_ref[0] == 0)
    def _():
        kept_ref[...], given_ref[...] = low, high

    @pl.when(core_ref[0] != 0)
    def _():
        kept_ref[...], given_ref[...] = high, low


def split_rows(core, recv, depth):
    n_src, rows, width = recv.shape
    out = jax.ShapeDtypeStruct((width // 2, n_src * CAP), recv.dtype)
    out_spec = pl.BlockSpec((depth // 2, n_src * CAP), lambda k: (k, 0))
    return pl.pallas_call(
        split_kernel,
        grid=(width // depth,),
        in_specs=[
            pl.BlockSpec(memory_space=pltpu.SMEM),
            pl.BlockSpec((n_src, rows, depth), lambda k: (0, 0, k)),
        ],
        out_specs=[out_spec, out_spec],
        out_shape=[out, out],
        name="split_rows",
    )(core.reshape(1), recv)


def pack_kernel(gu_ref, down_ref, out_ref):
    n_zl, n_yl, _, lanes = out_ref.shape
    gu_cols = gu_ref.shape[1]
    for j in range(n_yl):
        half = slice(j * lanes, (j + 1) * lanes)
        gu_t = gu_ref[half, :].T
        for i in range(n_zl):
            out_ref[i, j, :gu_cols, :] = gu_t
            out_ref[i, j, gu_cols:, :] = down_ref[:, half]


def pack_weights(gate_up, down, n_zl, n_yl):
    shape = (n_zl, n_yl, gate_up.shape[1] + down.shape[0], LANE)
    out = pl.pallas_call(pack_kernel, out_shape=jax.ShapeDtypeStruct(shape, gate_up.dtype), name="pack_weights")(
        gate_up, down
    )
    return out.reshape(n_zl * n_yl, shape[2], LANE)


def order_kernel(w_ref, gu_ref, down_ref):
    n_zl, n_yl, units, lanes = w_ref.shape
    hid = units // 3
    for i in range(n_zl):
        cols = slice(i * lanes, (i + 1) * lanes)
        for j in range(n_yl):
            gu_ref[2 * j * hid : 2 * (j + 1) * hid, cols] = w_ref[i, j, : 2 * hid, :]
            down_ref[j * hid : (j + 1) * hid, cols] = w_ref[i, j, 2 * hid :, :]


def order_weights(w_all):
    n_xc, n_zl, n_yl, units, lanes = w_all.shape
    hid = units // 3
    gu_rows, down_rows, cols = 2 * hid * n_yl, hid * n_yl, n_zl * lanes
    return pl.pallas_call(
        order_kernel,
        grid=(n_xc,),
        in_specs=[pl.BlockSpec((None, n_zl, n_yl, units, lanes), lambda k: (k, 0, 0, 0, 0))],
        out_specs=[pl.BlockSpec((gu_rows, cols), lambda k: (0, k)), pl.BlockSpec((down_rows, cols), lambda k: (0, k))],
        out_shape=[
            jax.ShapeDtypeStruct((gu_rows, n_xc * cols), w_all.dtype),
            jax.ShapeDtypeStruct((down_rows, n_xc * cols), w_all.dtype),
        ],
        name="order_weights",
    )(w_all)


def rows_kernel(n_zl, tokens_ref, dy_ref, slot_ref, gate_ref, out_ref):
    n_win, n_yl, n_zh, _, half = out_ref.shape
    n_tok = tokens_ref.shape[0]
    n_xc = half // (n_zl * LANE)
    positions = lax.broadcasted_iota(jnp.int32, (CAP, n_tok), 0)
    for e in range(n_win):
        picked = jnp.broadcast_to(slot_ref[e : e + 1, :], (CAP, n_tok)) == positions
        gate = jnp.sum(jnp.where(picked, gate_ref[e : e + 1, :], 0.0), axis=1, keepdims=True)
        one_hot = picked.astype(jnp.float32).astype(tokens_ref.dtype)
        x = jnp.dot(one_hot, tokens_ref[...], preferred_element_type=jnp.float32)
        g = jnp.dot(one_hot, dy_ref[...], preferred_element_type=jnp.float32) * gate
        both = jnp.concatenate([x, g], axis=0).astype(out_ref.dtype)
        for h in range(n_yl):
            for xc in range(n_xc):
                for zl in range(n_zl):
                    src = ((zl * n_xc + xc) * n_yl + h) * LANE
                    dst = (xc * n_zl + zl) * LANE
                    piece = both[:, src : src + LANE]
                    for zh in range(n_zh):
                        out_ref[e, h, zh, :, dst : dst + LANE] = piece


def select_rows(tokens, dy, slot_t, gate_t, n_zl, n_yl, n_zh):
    n_win, width = slot_t.shape[0], tokens.shape[1]
    shape = (n_win, n_yl, n_zh, 2 * CAP, width // n_yl)
    return pl.pallas_call(
        lambda *refs: rows_kernel(n_zl, *refs), out_shape=jax.ShapeDtypeStruct(shape, tokens.dtype), name="select_rows"
    )(tokens, dy, slot_t, gate_t)


def on_device(tokens, output_gradient, slot, gate_weight, gate_up_weight, down_weight):
    n_win = slot.shape[1]
    width = tokens.shape[1]
    n_half = width // (2 * LANE)
    hid = down_weight.shape[1]
    n_yl, n_zh, n_c = lax.axis_size("yl"), lax.axis_size("zh"), lax.axis_size("c")

    n_zl = lax.axis_size("zl")
    n_xc = n_half // n_zl
    rows = select_rows(tokens, output_gradient, jnp.transpose(slot), jnp.transpose(gate_weight), n_zl, n_yl, n_zh)
    rows = rows.reshape(-1, 2 * CAP, n_half * LANE)

    w_pair = a2a(pack_weights(gate_up_weight[0], down_weight[0], n_zl, n_yl), ("zl", "yl"))
    rows, w_pair = lax.optimization_barrier((rows, w_pair))
    w_all = lax.all_gather(w_pair.reshape(-1, LANE), ("x", "c"), axis=0, tiled=True)
    w_all = w_all.reshape(n_xc, n_zl, n_yl, 3 * hid, LANE)
    gu_cols = 2 * n_yl * hid
    w_gu_t, w_down_t = order_weights(w_all)
    recv, w_gu_t, w_down_t = lax.optimization_barrier((a2a(rows, EXPERT), w_gu_t, w_down_t))
    n_src = recv.shape[0]
    x_mat = recv[:, :CAP].reshape(n_src * CAP, n_half * LANE)
    g_mat = recv[:, CAP:].reshape(n_src * CAP, n_half * LANE)

    part = jnp.concatenate(
        [f32_dot(x_mat, w_gu_t, ((1,), (1,))), f32_dot(g_mat, w_down_t, ((1,), (1,)))], axis=1
    ).astype(jnp.bfloat16)

    part, recv = lax.optimization_barrier((part, recv))
    xt_kept, xt_given = split_rows(lax.axis_index("c"), recv, n_c * n_zl * LANE)
    part_other, xt_kept, xt_got = lax.optimization_barrier((swap(part, "yl"), xt_kept, swap(xt_given, "c")))

    total = part.astype(jnp.float32) + part_other.astype(jnp.float32)
    dgu = []
    for i in range(n_yl):
        pre, up = total[:, 2 * i * hid : (2 * i + 1) * hid], total[:, (2 * i + 1) * hid : (2 * i + 2) * hid]
        dh = total[:, gu_cols + i * hid : gu_cols + (i + 1) * hid]
        sig = jax.nn.sigmoid(pre)
        dgu += [dh * up * sig * (1.0 + pre * (1.0 - sig)), dh * (pre * sig)]
    dgu = jnp.concatenate(dgu, axis=1).astype(jnp.bfloat16)

    dx = jnp.dot(dgu, w_gu_t, preferred_element_type=jnp.float32).astype(jnp.bfloat16)
    dx, dgu_other = lax.optimization_barrier((dx, swap(dgu, "c")))
    both = jnp.concatenate([dgu, dgu_other], axis=0)
    pgu = jnp.dot(jnp.concatenate([xt_kept, xt_got], axis=1), both, preferred_element_type=jnp.float32).astype(jnp.bfloat16)

    summed = lax.psum_scatter(pgu, "x", scatter_dimension=0, tiled=True)
    summed = jnp.transpose(summed.reshape(n_zl, LANE, n_yl, 2 * hid), (0, 2, 1, 3))
    summed = a2a(summed.reshape(n_zl * n_yl, LANE, 2 * hid), ("zl", "yl"))
    grad_gu = jnp.sum(summed.reshape(n_zl, n_yl * LANE, 2 * hid).astype(jnp.float32), axis=0)
    grad_gu = grad_gu.astype(jnp.bfloat16)[None]

    back = a2a(dx.reshape(n_src, CAP, n_half * LANE), EXPERT)
    back = jnp.sum(back.reshape(n_win, n_yl, n_zh, CAP, n_xc, n_zl, LANE).astype(jnp.float32), axis=2)
    back = jnp.transpose(back, (0, 2, 4, 3, 1, 5)).reshape(n_win, CAP, width)
    positions = jnp.arange(CAP, dtype=jnp.int32)
    selector = jnp.transpose(slot)[:, None, :] == positions[None, :, None]
    grad_tokens = jnp.einsum("ect,ecd->td", selector.astype(jnp.float32), back).astype(jnp.bfloat16)
    return grad_tokens, grad_gu


def solution(mesh):
    fine = Mesh(mesh.devices.reshape(2, 4, 2, 4, 2, 4), FINE)
    dp, ex = FINE[:3], FINE[3:]
    in_specs = (P(FINE, None), P(FINE, None), P(FINE, None), P(FINE, None), P(ex, dp, None), P(ex, None, dp))
    out_specs = (P(FINE, None), P(ex, dp, None))
    return jax.shard_map(on_device, mesh=fine, in_specs=in_specs, out_specs=out_specs, check_vma=False)
```

```python
import jax
import jax.numpy as jnp
from jax import lax
from jax.experimental import pallas as pl
from jax.sharding import Mesh, PartitionSpec as P

FINE = ("zl", "x", "c", "yh", "yl", "zh")
EXPERT = ("yh", "yl", "zh")
CAP = 8
LANE = 128


def f32_dot(a, b, dims):
    return lax.dot_general(a, b, (dims, ((), ())), preferred_element_type=jnp.float32)


def a2a(v, axes):
    return lax.all_to_all(v, axes, split_axis=0, concat_axis=0, tiled=True)


def swap(v, axis):
    return lax.ppermute(v, axis, [(0, 1), (1, 0)])


def pack_kernel(gu_ref, down_ref, out_ref):
    n_zl, n_yl, _, lanes = out_ref.shape
    gu_cols = gu_ref.shape[1]
    for j in range(n_yl):
        half = slice(j * lanes, (j + 1) * lanes)
        gu_t = gu_ref[half, :].T
        for i in range(n_zl):
            out_ref[i, j, :gu_cols, :] = gu_t
            out_ref[i, j, gu_cols:, :] = down_ref[:, half]


def pack_weights(gate_up, down, n_zl, n_yl):
    shape = (n_zl, n_yl, gate_up.shape[1] + down.shape[0], LANE)
    out = pl.pallas_call(pack_kernel, out_shape=jax.ShapeDtypeStruct(shape, gate_up.dtype), name="pack_weights")(
        gate_up, down
    )
    return out.reshape(n_zl * n_yl, shape[2], LANE)


def order_kernel(w_ref, gu_ref, down_ref):
    n_zl, n_yl, units, lanes = w_ref.shape
    hid = units // 3
    for i in range(n_zl):
        cols = slice(i * lanes, (i + 1) * lanes)
        for j in range(n_yl):
            gu_ref[2 * j * hid : 2 * (j + 1) * hid, cols] = w_ref[i, j, : 2 * hid, :]
            down_ref[j * hid : (j + 1) * hid, cols] = w_ref[i, j, 2 * hid :, :]


def order_weights(w_all):
    n_xc, n_zl, n_yl, units, lanes = w_all.shape
    hid = units // 3
    gu_rows, down_rows, cols = 2 * hid * n_yl, hid * n_yl, n_zl * lanes
    return pl.pallas_call(
        order_kernel,
        grid=(n_xc,),
        in_specs=[pl.BlockSpec((None, n_zl, n_yl, units, lanes), lambda k: (k, 0, 0, 0, 0))],
        out_specs=[pl.BlockSpec((gu_rows, cols), lambda k: (0, k)), pl.BlockSpec((down_rows, cols), lambda k: (0, k))],
        out_shape=[
            jax.ShapeDtypeStruct((gu_rows, n_xc * cols), w_all.dtype),
            jax.ShapeDtypeStruct((down_rows, n_xc * cols), w_all.dtype),
        ],
        name="order_weights",
    )(w_all)


def rows_kernel(n_zl, tokens_ref, dy_ref, slot_ref, gate_ref, out_ref):
    n_win, n_yl, n_zh, _, half = out_ref.shape
    n_tok = tokens_ref.shape[0]
    n_xc = half // (n_zl * LANE)
    positions = lax.broadcasted_iota(jnp.int32, (CAP, n_tok), 0)
    for e in range(n_win):
        picked = jnp.broadcast_to(slot_ref[e : e + 1, :], (CAP, n_tok)) == positions
        gate = jnp.sum(jnp.where(picked, gate_ref[e : e + 1, :], 0.0), axis=1, keepdims=True)
        one_hot = picked.astype(jnp.float32).astype(tokens_ref.dtype)
        x = jnp.dot(one_hot, tokens_ref[...], preferred_element_type=jnp.float32)
        g = jnp.dot(one_hot, dy_ref[...], preferred_element_type=jnp.float32) * gate
        both = jnp.concatenate([x, g], axis=0).astype(out_ref.dtype)
        for h in range(n_yl):
            for xc in range(n_xc):
                for zl in range(n_zl):
                    src = ((zl * n_xc + xc) * n_yl + h) * LANE
                    dst = (xc * n_zl + zl) * LANE
                    piece = both[:, src : src + LANE]
                    for zh in range(n_zh):
                        out_ref[e, h, zh, :, dst : dst + LANE] = piece


def select_rows(tokens, dy, slot_t, gate_t, n_zl, n_yl, n_zh):
    n_win, width = slot_t.shape[0], tokens.shape[1]
    shape = (n_win, n_yl, n_zh, 2 * CAP, width // n_yl)
    return pl.pallas_call(
        lambda *refs: rows_kernel(n_zl, *refs), out_shape=jax.ShapeDtypeStruct(shape, tokens.dtype), name="select_rows"
    )(tokens, dy, slot_t, gate_t)


def on_device(tokens, output_gradient, slot, gate_weight, gate_up_weight, down_weight):
    n_win = slot.shape[1]
    width = tokens.shape[1]
    n_half = width // (2 * LANE)
    hid = down_weight.shape[1]
    n_yl, n_zh = lax.axis_size("yl"), lax.axis_size("zh")

    n_zl = lax.axis_size("zl")
    n_xc = n_half // n_zl
    rows = select_rows(tokens, output_gradient, jnp.transpose(slot), jnp.transpose(gate_weight), n_zl, n_yl, n_zh)
    rows = rows.reshape(-1, 2 * CAP, n_half * LANE)

    w_pair = a2a(pack_weights(gate_up_weight[0], down_weight[0], n_zl, n_yl), ("zl", "yl"))
    rows, w_pair = lax.optimization_barrier((rows, w_pair))
    w_all = lax.all_gather(w_pair.reshape(-1, LANE), ("x", "c"), axis=0, tiled=True)
    w_all = w_all.reshape(n_xc, n_zl, n_yl, 3 * hid, LANE)
    gu_cols = 2 * n_yl * hid
    w_gu_t, w_down_t = order_weights(w_all)
    recv, w_gu_t, w_down_t = lax.optimization_barrier((a2a(rows, EXPERT), w_gu_t, w_down_t))
    n_src = recv.shape[0]
    x_mat = recv[:, :CAP].reshape(n_src * CAP, n_half * LANE)
    g_mat = recv[:, CAP:].reshape(n_src * CAP, n_half * LANE)

    part = jnp.concatenate(
        [f32_dot(x_mat, w_gu_t, ((1,), (1,))), f32_dot(g_mat, w_down_t, ((1,), (1,)))], axis=1
    ).astype(jnp.bfloat16)

    total = part.astype(jnp.float32) + swap(part, "yl").astype(jnp.float32)
    dgu = []
    for i in range(n_yl):
        pre, up = total[:, 2 * i * hid : (2 * i + 1) * hid], total[:, (2 * i + 1) * hid : (2 * i + 2) * hid]
        dh = total[:, gu_cols + i * hid : gu_cols + (i + 1) * hid]
        sig = jax.nn.sigmoid(pre)
        dgu += [dh * up * sig * (1.0 + pre * (1.0 - sig)), dh * (pre * sig)]
    dgu = jnp.concatenate(dgu, axis=1).astype(jnp.bfloat16)

    pgu = [f32_dot(x_mat, dgu[:, 2 * i * hid : 2 * (i + 1) * hid], ((0,), (0,))) for i in range(n_yl)]
    pgu = jnp.stack([p.astype(jnp.bfloat16).reshape(n_half, LANE, 2 * hid) for p in pgu], axis=1).reshape(-1, 2 * hid)
    dx = jnp.dot(dgu, w_gu_t, preferred_element_type=jnp.float32).astype(jnp.bfloat16)

    summed = lax.psum_scatter(pgu, ("x", "c"), scatter_dimension=0, tiled=True)
    summed = a2a(summed.reshape(n_zl * n_yl, LANE, 2 * hid), ("zl", "yl"))
    grad_gu = jnp.sum(summed.reshape(n_zl, n_yl * LANE, 2 * hid).astype(jnp.float32), axis=0)
    grad_gu = grad_gu.astype(jnp.bfloat16)[None]

    back = a2a(dx.reshape(n_src, CAP, n_half * LANE), EXPERT)
    back = jnp.sum(back.reshape(n_win, n_yl, n_zh, CAP, n_xc, n_zl, LANE).astype(jnp.float32), axis=2)
    back = jnp.transpose(back, (0, 2, 4, 3, 1, 5)).reshape(n_win, CAP, width)
    positions = jnp.arange(CAP, dtype=jnp.int32)
    selector = jnp.transpose(slot)[:, None, :] == positions[None, :, None]
    grad_tokens = jnp.einsum("ect,ecd->td", selector.astype(jnp.float32), back).astype(jnp.bfloat16)
    return grad_tokens, grad_gu


def solution(mesh):
    fine = Mesh(mesh.devices.reshape(2, 4, 2, 4, 2, 4), FINE)
    dp, ex = FINE[:3], FINE[3:]
    in_specs = (P(FINE, None), P(FINE, None), P(FINE, None), P(FINE, None), P(ex, dp, None), P(ex, None, dp))
    out_specs = (P(FINE, None), P(ex, dp, None))
    return jax.shard_map(on_device, mesh=fine, in_specs=in_specs, out_specs=out_specs, check_vma=False)
```
